256 devices in a mesh: ang: 64 (over x, y, z_hi), rad: 4 (over z_lo, core).
Axes of the slice: x: 4, y: 4, z: 8 (z_hi: 4, z_lo: 2; z = z_hi * 2 + z_lo), core: 2. Of those that a mesh axis runs over, the one named last changes fastest.
Arguments:
- coarse: float32 [1, 64, 32, 512], P(None, 'ang', None, 'rad'), may hold values from -6 to 6
- excite: float32 [1, 128, 64, 1024], P(None, 'ang', None, 'rad'), may hold values from -6 to 6
- kernels: float32 [27, 8, 512], replicated, may hold values from -0.875 to 0.875
- mixing: float32 [8, 8, 512], replicated, may hold values from -1.5 to 1.5
- star_bin: int32 [128, 64, 16], P('ang'), may hold values from 0 to 1023
- star_count: int32 [128, 64], P('ang'), may hold values from 1 to 16
- star_obs: float32 [128, 64, 16], P('ang'), may hold values from 0 to 3
- star_isig: float32 [128, 64, 16], P('ang'), may hold values from 1 to 10
Outputs:
- grad_excite: float32 [1, 128, 64, 1024], P(None, 'ang', None, 'rad')
- grad_coarse: float32 [1, 64, 32, 512], P(None, 'ang', None, 'rad')
The draws below stay inside these ranges and needn't reach their ends.
All inputs are finite; a program needn't handle non-finite values.
Results may differ from the reference program's by a relative error of at most 0.0003.
Values sent between devices are 32-bit elements; how exact they have to be, the bound alone decides.
No kernel may reach another device: no remote copies, remote signals or barrier semaphores. Data moves between devices by JAX's collectives and lax.ppermute only.
A program may use at most 64 MiB of HBM per device.

```python
import math
import jax
import jax.numpy as jnp
from jax import lax

S = 1
CB = 32
MSTAR = 16
NAC = 64
NRC = 512
NA = 128
NB = 64
NR = 1024


def plant(values, key, low, top_value):
    longest = values.shape.index(max(values.shape))
    spots = []
    for shift in (0, 1):
        where = [jax.random.randint(jax.random.fold_in(key, axis), (), 0, length) for axis, length in enumerate(values.shape)]
        where[longest] = (where[longest] + shift) % values.shape[longest]
        spots.append(tuple(where))
    return values.at[spots[0]].set(low).at[spots[1]].set(top_value)


def block_levels(stream_key, shape, shards, smallest, top_value):
    loudness, own = 1.0, jax.random.fold_in(stream_key, 6)
    for position, blocks in shards:
        steps = jnp.exp(jax.random.uniform(jax.random.fold_in(own, position), (blocks,), jnp.float32, smallest / len(shards), top_value / len(shards)))
        loudness = loudness * jnp.repeat(steps, shape[position] // blocks).reshape([-1 if axis == position else 1 for axis in range(len(shape))])
    return loudness


def gaussian(key, shape, spread, limit, shards=(), kind=jnp.bfloat16):
    drawn = spread * jax.random.normal(key, shape, jnp.float32)
    if shards:
        drawn = drawn * block_levels(key, shape, shards, -0.22, 0.18)
    return jnp.clip(drawn, -limit, limit).astype(kind)


def setup_inputs(seed: int = 0) -> dict:
    streams_of = jax.random.split(jax.random.key(seed), 9)
    coarse = gaussian(streams_of[0], (S, NAC, CB, NRC), 1.0, 6.0, ((1, 64), (3, 4)), jnp.float32)
    excite = gaussian(streams_of[1], (S, NA, NB, NR), 1.0, 6.0, ((1, 64), (3, 4)), jnp.float32)
    kernels = gaussian(streams_of[2], (27, 8, NRC), 54 ** -0.5, 0.875, (), jnp.float32)
    mixing = gaussian(streams_of[3], (8, 8, NRC), 16 ** -0.5, 1.5, (), jnp.float32)
    star_bin = plant(jax.random.randint(streams_of[4], (NA, NB, MSTAR), 0, NR), jax.random.fold_in(streams_of[4], 1), 0, NR - 1).astype(jnp.int32)
    star_count = plant(jax.random.randint(streams_of[5], (NA, NB), 1, MSTAR + 1), jax.random.fold_in(streams_of[5], 1), 1, MSTAR).astype(jnp.int32)
    star_obs = jnp.clip(3.0 * jax.random.uniform(streams_of[6], (NA, NB, MSTAR), jnp.float32) ** block_levels(streams_of[6], (NA, NB, MSTAR), ((0, 64),), -0.2, 0.2), 0.0, 3.0)
    star_isig = jnp.clip(jnp.exp(math.log(10.0) - 2.3025851 * jax.random.uniform(streams_of[7], (NA, NB, MSTAR), jnp.float32) ** block_levels(streams_of[7], (NA, NB, MSTAR), ((0, 64),), -0.2, 0.2)), 1.0, 10.0)
    return {"coarse": coarse, "excite": excite, "kernels": kernels, "mixing": mixing, "star_bin": star_bin, "star_count": star_count, "star_obs": star_obs, "star_isig": star_isig}


def to_blocks(field):
    na, nb, nr = field.shape
    return field.reshape(na // 2, 2, nb // 2, 2, nr // 2, 2).transpose(1, 3, 5, 0, 2, 4).reshape(8, na // 2, nb // 2, nr // 2)


def from_blocks(blocks):
    _, na, nb, nr = blocks.shape
    return blocks.reshape(2, 2, 2, na, nb, nr).transpose(3, 0, 4, 1, 5, 2).reshape(2 * na, 2 * nb, 2 * nr)


def one_sample(coarse, excite, kernels, mixing, star_bin, star_count, star_obs, star_isig):
    na, nb, nr = coarse.shape
    padded = jnp.pad(coarse, 1)
    fine = jnp.zeros((8, na, nb, nr), jnp.float32)
    for offset in range(27):
        step_a, step_b, step_r = offset // 9, (offset // 3) % 3, offset % 3
        window = padded[step_a:step_a + na, step_b:step_b + nb, step_r:step_r + nr]
        fine = fine + kernels[offset][:, None, None, :] * window[None]
    excite_blocks = to_blocks(excite)
    fine = fine + jnp.einsum("qpr,pabr->qabr", mixing, excite_blocks, precision=lax.Precision.HIGHEST)
    dens = jnp.exp(from_blocks(fine))
    step_len = 1.0 / NR
    extinction = step_len * jnp.cumsum(dens, axis=2)
    pred = jnp.take_along_axis(extinction, star_bin, axis=2)
    live = jnp.arange(MSTAR)[None, None, :] < star_count[:, :, None]
    res = jnp.where(live, (pred - star_obs) * star_isig, 0.0)
    terms = res * star_isig
    rows_a = jnp.broadcast_to(jnp.arange(NA)[:, None, None], star_bin.shape)
    rows_b = jnp.broadcast_to(jnp.arange(NB)[None, :, None], star_bin.shape)
    hits = jnp.zeros((NA, NB, NR), jnp.float32).at[rows_a, rows_b, star_bin].add(terms)
    suffix = jnp.flip(jnp.cumsum(jnp.flip(hits, 2), axis=2), 2)
    grad_fine = to_blocks(dens * step_len * suffix)
    grad_excite = from_blocks(jnp.einsum("qpr,qabr->pabr", mixing, grad_fine, precision=lax.Precision.HIGHEST) + excite_blocks)
    summed = jnp.zeros((na + 2, nb + 2, nr + 2), jnp.float32)
    for offset in range(27):
        step_a, step_b, step_r = offset // 9, (offset // 3) % 3, offset % 3
        contrib = jnp.sum(kernels[offset][:, None, None, :] * grad_fine, axis=0)
        summed = summed.at[step_a:step_a + na, step_b:step_b + nb, step_r:step_r + nr].add(contrib)
    return grad_excite, summed[1:-1, 1:-1, 1:-1]


def reference(coarse, excite, kernels, mixing, star_bin, star_count, star_obs, star_isig):
    def single(pair):
        return one_sample(pair[0], pair[1], kernels, mixing, star_bin, star_count, star_obs, star_isig)

    grad_excite, grad_coarse = lax.map(single, (coarse, excite))
    return grad_excite, grad_coarse
```

```python
import jax
import jax.numpy as jnp
from jax import lax
from jax.experimental import pallas as pl
from jax.experimental.pallas import tpu as pltpu
from jax.sharding import PartitionSpec as P

F32 = jnp.float32
HI = lax.Precision.HIGHEST
VMEM = pl.BlockSpec(memory_space=pltpu.VMEM)


def lanes(shape):
    return lax.broadcasted_iota(jnp.int32, shape, 1)


def rows(shape):
    return lax.broadcasted_iota(jnp.int32, shape, 0)


def along(x, k, axis):
    if k == 0:
        return x
    n = x.shape[axis]
    at = lax.broadcasted_iota(jnp.int32, x.shape, axis)
    inside = at < n - k if k > 0 else at >= -k
    return jnp.where(inside, pltpu.roll(x, (-k) % n, axis), 0.0)


def pick(x, index):
    return jnp.take_along_axis(x, index, axis=1, mode="promise_in_bounds")


def wide(x):
    return jnp.concatenate([x, jnp.zeros((x.shape[0], 128 - x.shape[1]), x.dtype)], axis=1)


def split_pixels(ref, j):
    half = pl.ds(j, 32, stride=2)
    low, high = ref[0, half, :], ref[1, half, :]
    lane = lanes((32, 128))
    out = []
    for k in range(2):
        index = (2 * lane + k) & 127
        out.append(jnp.where(lane < 64, pick(low, index), pick(high, index)))
    return out


def taps(acc, row, weights, first, shard):
    here = pl.ds(pl.multiple_of(shard * 128, 128), 128)
    for w in range(3):
        moved = along(row, w - 1, 1)
        for v in range(3):
            window = along(moved, v - 1, 0)
            t = first + 3 * v + w
            block = weights[t, :, here]
            for q in range(8):
                acc[q] = acc[q] + block[q : q + 1, :] * window


def prepare(coarse, excite, kernels, mixing, star_bin, star_count, star_obs, star_isig,
            base, fields, rel_out, w_out, o_out, sums, count_t, halves, slots, bins):
    shard = lax.axis_index("rad")
    here = pl.ds(pl.multiple_of(shard * 128, 128), 128)
    parts = []
    for i in range(2):
        halves[i, 0] = excite[i, :, 0:128]
        halves[i, 1] = excite[i, :, 128:256]
        bins[i] = wide(star_bin[i])
        slots[i, 0] = wide(star_isig[i])
        slots[i, 1] = wide(star_obs[i])
    for i in range(2):
        for j in range(2):
            parts += split_pixels(halves.at[i], j)
    for p in range(8):
        fields[p] = parts[p]
    acc = []
    for q in range(8):
        block = mixing[q, :, here]
        total = block[0:1, :] * parts[0]
        for p in range(1, 8):
            total = total + block[p : p + 1, :] * parts[p]
        acc.append(total)
    taps(acc, coarse[...], kernels, 9, shard)
    for q in range(8):
        base[q] = acc[q]
    counts = jnp.concatenate([star_count[...].astype(F32), jnp.zeros((2, 64), F32)], axis=1)
    counts = jnp.concatenate([counts, jnp.zeros((126, 128), F32)], axis=0)
    count_t[...] = counts.T
    lane = lanes((32, 128))
    table = jnp.zeros((32, 128), F32)
    for i in range(2):
        for j in range(2):
            p = 2 * i + j
            half = pl.ds(j, 32, stride=2)
            count = count_t[half, :][:, i : i + 1]
            rel = bins[i, half, :] - 256 * shard
            live = (lane < 16) & (lane.astype(F32) < count) & (rel >= 0) & (rel < 256)
            isig = slots[i, 0, half, :]
            w = jnp.where(live, isig * isig, 0.0)
            o = w * slots[i, 1, half, :]
            rel = jnp.where(live, rel, -1)
            rel_out[p] = rel
            w_out[p] = w
            o_out[p] = o
            for k in range(2):
                for group, least in ((40, k), (48, 254 + k)):
                    deep = rel >= least
                    total = jnp.sum(jnp.where(deep, w, 0.0), axis=1, keepdims=True)
                    table = jnp.where(lane == group + 2 * p + k, total, table)
                    total = jnp.sum(jnp.where(deep, o, 0.0), axis=1, keepdims=True)
                    table = jnp.where(lane == group + 16 + 2 * p + k, total, table)
    sums[...] = table


def forward(coarse, low, high, base, kernels, rel_in, w_in, o_in, sums, dens, local, table):
    shard = lax.axis_index("rad")
    step = 1.0 / 1024
    acc = [base[q] for q in range(8)]
    taps(acc, low[...], kernels, 0, shard)
    taps(acc, high[...], kernels, 18, shard)
    lane = lanes((32, 128))
    out = sums[...]
    for q in range(8):
        out = jnp.where(lane == q, acc[q][:, 0:1], out)
        out = jnp.where(lane == 8 + q, acc[q][:, 127:128], out)
    for u, row in enumerate((low, coarse, high)):
        value = row[...]
        out = jnp.where(lane == 32 + u, value[:, 0:1], out)
        out = jnp.where(lane == 35 + u, value[:, 127:128], out)
    inner = (lane > 0) & (lane < 127)
    density = []
    for q in range(8):
        d = jnp.exp(acc[q])
        dens[q] = d
        density.append(jnp.where(inner, d, 0.0))
    pairs = jnp.concatenate([density[2 * p] + density[2 * p + 1] for p in range(4)], axis=0)
    strict = (rows((128, 128)) < lanes((128, 128))).astype(F32)
    before = jnp.dot(pairs, strict, precision=HI, preferred_element_type=F32)
    for p in range(4):
        first = before[32 * p : 32 * p + 32] + density[2 * p]
        second = first + density[2 * p + 1]
        rel = jnp.maximum(rel_in[p], 0)
        index = rel >> 1
        at = jnp.where((rel & 1) == 1, pick(second, index), pick(first, index))
        local[p] = at
        total = second[:, 127:128]
        share = jnp.sum(step * at * w_in[p] - o_in[p], axis=1, keepdims=True)
        for k in range(2):
            out = jnp.where(lane == 16 + 2 * p + k, total, out)
            out = jnp.where(lane == 24 + 2 * p + k, share, out)
    table[...] = out


def swap(x):
    even = (rows(x.shape) & 1) == 0
    return jnp.where(even, pltpu.roll(x, x.shape[0] - 1, 0), pltpu.roll(x, 1, 0))


def backward(table, dens, local, kernels, rel_in, w_in, o_in, grad, to_low, own, to_high):
    shard = lax.axis_index("rad")
    step = 1.0 / 1024
    even = (rows((8, 128)) & 1) == 0
    groups = []
    for s in range(4):
        full = jnp.concatenate([table[s], jnp.zeros((96, 128), F32)], axis=0).T
        groups.append([full[8 * g : 8 * g + 8] for g in range(9)])
    edges = []
    for s in range(4):
        e = groups[s][4]
        edges.append([along(e, v - 1, 1) for v in range(3)])
    d_low, d_high, totals, shares, whole = [], [], [], [], []
    for s in range(4):
        f_low, f_high, t, c, _, w_low, w_high, o_low, o_high = groups[s]
        for u in range(3):
            for v in range(3):
                if s > 0:
                    weight = kernels[9 * u + 3 * v, :, 128 * s : 128 * s + 128][:, 0:1]
                    f_low = f_low + weight * edges[s - 1][v][3 + u : 4 + u, :]
                if s < 3:
                    weight = kernels[9 * u + 3 * v + 2, :, 128 * s : 128 * s + 128][:, 127:128]
                    f_high = f_high + weight * edges[s + 1][v][u : u + 1, :]
        a, b = jnp.exp(f_low), jnp.exp(f_high)
        d_low.append(a)
        d_high.append(b)
        both = a + b
        totals.append(t + both + swap(both))
        both = a * w_low + b * w_high
        shares.append(c + step * (both + swap(both)))
        whole.append(jnp.where(even, w_low, swap(w_low)))
    zero = jnp.zeros((8, 128), F32)
    nearer = [zero]
    for s in range(3):
        nearer.append(nearer[s] + totals[s])
    nearer = [step * x for x in nearer]
    sums = [shares[s] + nearer[s] * whole[s] for s in range(4)]
    farther = [zero]
    for s in (3, 2, 1):
        farther.insert(0, farther[0] + sums[s])

    def low_edge(s):
        _, _, _, _, _, w, _, o, _ = groups[s]
        first = (nearer[s] + step * swap(d_low[s])) * (swap(w) - w) - (swap(o) - o)
        suffix = sums[s] - jnp.where(even, 0.0, first)
        return d_low[s] * step * (farther[s] + suffix)

    def high_edge(s):
        _, _, _, _, _, _, w, _, o = groups[s]
        last = step * swap(d_high[s]) * (w - swap(w))
        suffix = (nearer[s] + step * totals[s]) * w - o - jnp.where(even, last, 0.0)
        return d_high[s] * step * (farther[s] + suffix)

    def mine(values):
        out = values[0]
        for s in range(1, 4):
            out = jnp.where(shard == s, values[s], out)
        return out

    columns = [mine(d_low), mine(d_high), mine(nearer), mine(farther),
               mine([zero, high_edge(0), high_edge(1), high_edge(2)]),
               mine([low_edge(1), low_edge(2), low_edge(3), zero])]
    columns = jnp.concatenate(columns + [jnp.zeros((80, 128), F32)], axis=0).T[0:32]

    def column(group, q):
        return columns[:, 8 * group + q : 8 * group + q + 1]

    lane = lanes((32, 128))
    plus, minus, here = [], [], []
    for p in range(4):
        a0, a1 = column(0, 2 * p), column(0, 2 * p + 1)
        b0, b1 = column(1, 2 * p), column(1, 2 * p + 1)
        rel = rel_in[p]
        reach = local[p] + jnp.where(rel >= 0, a0, 0.0) + jnp.where(rel >= 1, a1, 0.0)
        reach = reach + jnp.where(rel >= 254, b0, 0.0) + jnp.where(rel >= 255, b1, 0.0)
        term = w_in[p] * (column(2, 2 * p) + step * reach) - o_in[p]
        s0 = jnp.broadcast_to(column(3, 2 * p), (32, 128))
        s1 = s0
        for m in range(16):
            at = rel[:, m : m + 1]
            value = term[:, m : m + 1]
            s0 = s0 + jnp.where(at >= 2 * lane, value, 0.0)
            s1 = s1 + jnp.where(at > 2 * lane, value, 0.0)
        for k, s in ((0, s0), (1, s1)):
            q = 2 * p + k
            d = jnp.where(lane == 0, column(0, q), dens[q])
            d = jnp.where(lane == 127, column(1, q), d)
            g = d * step * s
            grad[q] = g
            here.append(g)
            plus.append(jnp.where(lane == 127, column(4, q), g))
            minus.append(jnp.where(lane == 0, column(5, q), g))
    at = pl.ds(pl.multiple_of(shard * 128, 128), 128)
    prev = pl.ds(pl.multiple_of(jnp.maximum(shard - 1, 0) * 128, 128), 128)
    after = pl.ds(pl.multiple_of(jnp.minimum(shard + 1, 3) * 128, 128), 128)
    lane8 = lanes((8, 128))
    for u, out in enumerate((to_low, own, to_high)):
        total = None
        for w, field in enumerate((minus, here, plus)):
            part = None
            for v in range(3):
                t = 9 * u + 3 * v + w
                block = kernels[t, :, at]
                if w == 0:
                    block = jnp.where(lane8 == 0, kernels[t, :, after], block)
                if w == 2:
                    block = jnp.where(lane8 == 127, kernels[t, :, prev], block)
                piece = block[0:1, :] * field[0]
                for q in range(1, 8):
                    piece = piece + block[q : q + 1, :] * field[q]
                piece = along(piece, 1 - v, 0)
                part = piece if part is None else part + piece
            if w != 1:
                part = pltpu.roll(part, (w - 1) % 128, 1)
            total = part if total is None else total + part
        out[...] = total


def finish(grad, fields, mixing, out, halves):
    shard = lax.axis_index("rad")
    at = pl.ds(pl.multiple_of(shard * 128, 128), 128)
    lane = lanes((32, 128))
    acc = [fields[p] for p in range(8)]
    for q in range(8):
        block = mixing[q, :, at]
        g = grad[q]
        for p in range(8):
            acc[p] = acc[p] + block[p : p + 1, :] * g
    for i in range(2):
        for j in range(2):
            pair = acc[4 * i + 2 * j : 4 * i + 2 * j + 2]
            half = pl.ds(j, 32, stride=2)
            for side in range(2):
                index = (lane >> 1) + 64 * side
                value = jnp.where((lane & 1) == 0, pick(pair[0], index), pick(pair[1], index))
                halves[side, half, :] = value
        for side in range(2):
            out[i, :, 128 * side : 128 * side + 128] = halves[side]


def call(body, name, ins, outs, flops, scratch=()):
    shapes = tuple(jax.ShapeDtypeStruct(s, d) for s, d in outs)
    size = sum(x.size * 4 for x in ins) + sum(x.size * 4 for x in shapes)
    return pl.pallas_call(
        body,
        name=name,
        out_shape=shapes,
        in_specs=[VMEM] * len(ins),
        out_specs=tuple([VMEM] * len(shapes)),
        scratch_shapes=list(scratch),
        cost_estimate=pl.CostEstimate(flops=flops, bytes_accessed=size, transcendentals=0),
        compiler_params=pltpu.CompilerParams(vmem_limit_bytes=16 << 20),
    )(*ins)


def per_device(coarse, excite, kernels, mixing, star_bin, star_count, star_obs, star_isig):
    count = lax.axis_size("ang")
    up = [(i, i + 1) for i in range(count - 1)]
    down = [(i + 1, i) for i in range(count - 1)]
    own = coarse[0, 0]
    low = lax.ppermute(own, "ang", up)
    high = lax.ppermute(own, "ang", down)
    block = ((8, 32, 128), F32)
    stars = ((4, 32, 128), F32)
    row = ((32, 128), F32)
    base, fields, rel, w, o, sums = call(
        prepare, "prepare",
        (own, excite[0], kernels, mixing, star_bin, star_count, star_obs, star_isig),
        (block, block, ((4, 32, 128), jnp.int32), stars, stars, row), 4_000_000,
        [pltpu.VMEM((128, 128), F32), pltpu.VMEM((2, 2, 64, 128), F32),
         pltpu.VMEM((2, 2, 64, 128), F32), pltpu.VMEM((2, 64, 128), jnp.int32)],
    )
    dens, local, table = call(
        forward, "forward", (own, low, high, base, kernels, rel, w, o, sums),
        (block, stars, row), 6_000_000,
    )
    tables = lax.all_gather(table, "rad")
    grad, to_low, here, to_high = call(
        backward, "backward", (tables, dens, local, kernels, rel, w, o),
        (block, row, row, row), 8_000_000,
    )
    from_high = lax.ppermute(to_low, "ang", down)
    from_low = lax.ppermute(to_high, "ang", up)
    (grad_excite,) = call(
        finish, "finish", (grad, fields, mixing), (((2, 64, 256), F32),), 4_000_000,
        [pltpu.VMEM((2, 64, 128), F32)],
    )
    grad_coarse = here + from_high + from_low
    return grad_excite[None], grad_coarse[None, None]


def solution(mesh):
    in_specs = (
        P(None, "ang", None, "rad"),
        P(None, "ang", None, "rad"),
        P(),
        P(),
        P("ang", None, None),
        P("ang", None),
        P("ang", None, None),
        P("ang", None, None),
    )
    out_specs = (P(None, "ang", None, "rad"), P(None, "ang", None, "rad"))
    return jax.shard_map(
        per_device, mesh=mesh, in_specs=in_specs, out_specs=out_specs, check_vma=False
    )
```

```python
import jax
import jax.numpy as jnp
from jax import lax
from jax.experimental import pallas as pl
from jax.experimental.pallas import tpu as pltpu
from jax.sharding import PartitionSpec as P


F32 = jnp.float32
HI = lax.Precision.HIGHEST
VMEM = pl.BlockSpec(memory_space=pltpu.VMEM)


def lanes(shape):
    return lax.broadcasted_iota(jnp.int32, shape, 1)


def rows(shape):
    return lax.broadcasted_iota(jnp.int32, shape, 0)


def along(x, k, axis):
    if k == 0:
        return x
    n = x.shape[axis]
    at = lax.broadcasted_iota(jnp.int32, x.shape, axis)
    inside = at < n - k if k > 0 else at >= -k
    return jnp.where(inside, pltpu.roll(x, (-k) % n, axis), 0.0)


def pick(x, index):
    return jnp.take_along_axis(x, index, axis=1, mode="promise_in_bounds")


def split_pixels(ref, j):
    half = pl.ds(j, 32, stride=2)
    low, high = ref[0, half, :], ref[1, half, :]
    lane = lanes((32, 128))
    out = []
    for k in range(2):
        index = (2 * lane + k) & 127
        out.append(jnp.where(lane < 64, pick(low, index), pick(high, index)))
    return out


def taps(acc, row, weights):
    for w in range(3):
        moved = along(row, w - 1, 1)
        for v in range(3):
            window = along(moved, v - 1, 0)
            block = weights[3 * v + w]
            for q in range(8):
                acc[q] = acc[q] + block[q : q + 1, :] * window


def prepare(coarse_in, excite_in, kernels_in, mixing_in, bin_in, count_in, obs_in, isig_in,
            base, fields, hits_w, deep_w, deep_o, sums, mixing,
            slots, halves, coarse, kernels, star_bin, star_count, star_obs, star_isig, arrived):
    shard = lax.axis_index("rad")
    here = pl.ds(pl.multiple_of(shard * 128, 128), 128)
    moves = [(bin_in, star_bin), (count_in, star_count), (obs_in, star_obs), (isig_in, star_isig)]
    for i in range(2):
        for side in range(2):
            moves.append((excite_in.at[i, :, 128 * side : 128 * side + 128], halves.at[i, side]))
    moves += [(mixing_in.at[:, :, here], mixing), (coarse_in, coarse), (kernels_in.at[9:18, :, here], kernels)]
    moves = [pltpu.make_async_copy(a, b, arrived.at[n]) for n, (a, b) in enumerate(moves)]
    for move in moves:
        move.start()
    for move in moves[:4]:
        move.wait()
    slot = rows((16, 64)).astype(F32)
    stack = []
    for i in range(2):
        count = star_count[i : i + 1, :].astype(F32)
        rel = (star_bin[i] - 256 * shard).astype(F32)
        live = (slot < count) & (rel >= 0.0) & (rel < 256.0)
        isig = star_isig[i]
        w = jnp.where(live, isig * isig, 0.0)
        stack += [jnp.where(live, rel, -1.0), w, w * star_obs[i]]
    stack = jnp.concatenate(stack + [jnp.zeros((32, 64), F32)], axis=0)
    slots[...] = jnp.concatenate([stack, jnp.zeros((128, 64), F32)], axis=1).T
    for move in moves[4:]:
        move.wait()
    parts = []
    for i in range(2):
        for j in range(2):
            parts += split_pixels(halves.at[i], j)
    for p in range(8):
        fields[p] = parts[p]
    acc = []
    for q in range(8):
        block = mixing[q]
        total = block[0:1, :] * parts[0]
        for p in range(1, 8):
            total = total + block[p : p + 1, :] * parts[p]
        acc.append(total)
    taps(acc, coarse[...], [kernels[t] for t in range(9)])
    for q in range(8):
        base[q] = acc[q]
    lane = lanes((32, 128))
    bin0 = 2.0 * lane.astype(F32)
    bin1 = bin0 + 1.0
    zero = jnp.zeros((32, 128), F32)
    hits = [[zero] * 8, [zero] * 8]
    for j in range(2):
        stars = slots[pl.ds(j, 32, stride=2), :]
        for i in range(2):
            q = 4 * i + 2 * j
            for m in range(16):
                at = 48 * i + m
                rel = stars[:, at : at + 1]
                is0, is1 = rel == bin0, rel == bin1
                for f in range(2):
                    value = stars[:, at + 16 + 16 * f : at + 17 + 16 * f]
                    hits[f][q] = hits[f][q] + jnp.where(is0, value, 0.0)
                    hits[f][q + 1] = hits[f][q + 1] + jnp.where(is1, value, 0.0)
    pairs = jnp.concatenate([hits[f][2 * p] + hits[f][2 * p + 1] for f in range(2) for p in range(4)], axis=0)
    beyond = (rows((128, 128)) > lanes((128, 128))).astype(F32)
    after = jnp.dot(pairs, beyond, precision=HI, preferred_element_type=F32)
    table = zero
    for f, out in ((0, deep_w), (1, deep_o)):
        for p in range(4):
            second = after[128 * f + 32 * p : 128 * f + 32 * p + 32] + hits[f][2 * p + 1]
            first = second + hits[f][2 * p]
            for k, value in ((0, first), (1, second)):
                q = 2 * p + k
                out[q] = value
                table = jnp.where(lane == 40 + 16 * f + q, value[:, 0:1], table)
                table = jnp.where(lane == 48 + 16 * f + q, value[:, 127:128], table)
    for q in range(8):
        hits_w[q] = hits[0][q]
    sums[...] = table


def sides(odd, even):
    first = (lax.axis_index("ang") & 1) == 0
    return jnp.where(first, odd, even), jnp.where(first, even, odd)


def forward(coarse, odd, even, base, kernels, hits_w, sums, dens, prod, table):
    shard = lax.axis_index("rad")
    step = 1.0 / 1024
    acc = [base[q] for q in range(8)]
    low, high = sides(odd[...], even[...])
    here = pl.ds(pl.multiple_of(shard * 128, 128), 128)
    taps(acc, low, [kernels[t, :, here] for t in range(9)])
    taps(acc, high, [kernels[t, :, here] for t in range(18, 27)])
    lane = lanes((32, 128))
    out = sums[...]
    for q in range(8):
        out = jnp.where(lane == q, acc[q][:, 0:1], out)
        out = jnp.where(lane == 8 + q, acc[q][:, 127:128], out)
    for u, value in enumerate((low, coarse[...], high)):
        out = jnp.where(lane == 32 + u, value[:, 0:1], out)
        out = jnp.where(lane == 35 + u, value[:, 127:128], out)
    inner = (lane > 0) & (lane < 127)
    density = []
    for q in range(8):
        d = jnp.exp(acc[q])
        dens[q] = d
        density.append(jnp.where(inner, d, 0.0))
    pairs = jnp.concatenate([density[2 * p] + density[2 * p + 1] for p in range(4)], axis=0)
    strict = (rows((128, 128)) < lanes((128, 128))).astype(F32)
    before = jnp.dot(pairs, strict, precision=HI, preferred_element_type=F32)
    for p in range(4):
        first = before[32 * p : 32 * p + 32] + density[2 * p]
        second = first + density[2 * p + 1]
        first = weighed(step * first, hits_w[2 * p])
        total = second[:, 127:128]
        second = weighed(step * second, hits_w[2 * p + 1])
        prod[2 * p] = first
        prod[2 * p + 1] = second
        share = jnp.sum(first + second, axis=1, keepdims=True)
        for k in range(2):
            out = jnp.where(lane == 16 + 2 * p + k, total, out)
            out = jnp.where(lane == 24 + 2 * p + k, share, out)
    table[...] = out


def weighed(x, w):
    return jnp.where(w != 0.0, x * w, 0.0)


def swap(x):
    even = (rows(x.shape) & 1) == 0
    return jnp.where(even, pltpu.roll(x, x.shape[0] - 1, 0), pltpu.roll(x, 1, 0))


def spread(grad, columns):
    lane = lanes((32, 128))
    plus, minus = [], []
    for q in range(8):
        plus.append(jnp.where(lane == 127, columns[:, 32 + q : 33 + q], grad[q]))
        minus.append(jnp.where(lane == 0, columns[:, 40 + q : 41 + q], grad[q]))
    return minus, grad, plus


def to_row(u, fields, kernels, shard):
    at = pl.ds(pl.multiple_of(shard * 128, 128), 128)
    prev = pl.ds(pl.multiple_of(jnp.maximum(shard - 1, 0) * 128, 128), 128)
    after = pl.ds(pl.multiple_of(jnp.minimum(shard + 1, 3) * 128, 128), 128)
    lane = lanes((8, 128))
    total = None
    for w, field in enumerate(fields):
        part = None
        for v in range(3):
            t = 9 * u + 3 * v + w
            block = kernels[t, :, at]
            if w == 0:
                block = jnp.where(lane == 0, kernels[t, :, after], block)
            if w == 2:
                block = jnp.where(lane == 127, kernels[t, :, prev], block)
            piece = block[0:1, :] * field[0]
            for q in range(1, 8):
                piece = piece + block[q : q + 1, :] * field[q]
            piece = along(piece, 1 - v, 0)
            part = piece if part is None else part + piece
        if w != 1:
            part = pltpu.roll(part, (w - 1) % 128, 1)
        total = part if total is None else total + part
    return total


def backward(table, dens, prod, kernels, deep_w, deep_o, grad, edges_out, odd_out, even_out):
    shard = lax.axis_index("rad")
    step = 1.0 / 1024
    even = (rows((8, 128)) & 1) == 0
    pairs = jnp.concatenate([prod[2 * p] + prod[2 * p + 1] for p in range(4)], axis=0)
    beyond = (rows((128, 128)) > lanes((128, 128))).astype(F32)
    after = jnp.dot(pairs, beyond, precision=HI, preferred_element_type=F32)
    groups = []
    for s in range(4):
        full = jnp.concatenate([table[s], jnp.zeros((96, 128), F32)], axis=0).T
        groups.append([full[8 * g : 8 * g + 8] for g in range(9)])
    edges = []
    for s in range(4):
        e = groups[s][4]
        edges.append([along(e, v - 1, 1) for v in range(3)])
    d_low, d_high, totals, shares, whole, tails = [], [], [], [], [], []
    for s in range(4):
        f_low, f_high, t, c, _, w_low, w_high, o_low, _ = groups[s]
        for u in range(3):
            for v in range(3):
                if s > 0:
                    weight = kernels[9 * u + 3 * v, :, 128 * s : 128 * s + 128][:, 0:1]
                    f_low = f_low + weight * edges[s - 1][v][3 + u : 4 + u, :]
                if s < 3:
                    weight = kernels[9 * u + 3 * v + 2, :, 128 * s : 128 * s + 128][:, 127:128]
                    f_high = f_high + weight * edges[s + 1][v][u : u + 1, :]
        a, b = jnp.exp(f_low), jnp.exp(f_high)
        d_low.append(a)
        d_high.append(b)
        both = a + b
        totals.append(t + both + swap(both))
        tail = step * b * w_high
        tail = tail + swap(tail)
        tails.append(tail)
        head = step * a * w_low
        o_all = jnp.where(even, o_low, swap(o_low))
        shares.append(c - o_all + head + swap(head) + tail)
        whole.append(jnp.where(even, w_low, swap(w_low)))
    zero = jnp.zeros((8, 128), F32)
    nearer = [zero]
    for s in range(3):
        nearer.append(nearer[s] + totals[s])
    nearer = [step * x for x in nearer]
    sums = [shares[s] + weighed(nearer[s], whole[s]) for s in range(4)]
    farther = [zero]
    for s in (3, 2, 1):
        farther.insert(0, farther[0] + sums[s])

    def low_edge(s):
        w, o = groups[s][5], groups[s][7]
        first = weighed(nearer[s] + step * swap(d_low[s]), swap(w) - w) - (swap(o) - o)
        suffix = sums[s] - jnp.where(even, 0.0, first)
        return d_low[s] * step * (farther[s] + suffix)

    def high_edge(s):
        w, o = groups[s][6], groups[s][8]
        last = step * swap(d_high[s]) * (w - swap(w))
        suffix = weighed(nearer[s] + step * totals[s], w) - o - jnp.where(even, last, 0.0)
        return d_high[s] * step * (farther[s] + suffix)

    def mine(values):
        out = values[0]
        for s in range(1, 4):
            out = jnp.where(shard == s, values[s], out)
        return out

    lows = [low_edge(s) for s in range(4)]
    highs = [high_edge(s) for s in range(4)]
    columns = [mine(lows), mine(highs),
               mine([nearer[s] + step * (d_low[s] + swap(d_low[s])) for s in range(4)]),
               mine([farther[s] + tails[s] for s in range(4)]),
               mine([zero] + highs[:3]), mine(lows[1:] + [zero])]
    columns = jnp.concatenate(columns + [jnp.zeros((80, 128), F32)], axis=0).T[0:32]
    edges_out[...] = columns
    lane = lanes((32, 128))
    grads = []
    for p in range(4):
        near, far = columns[:, 16 + 2 * p : 17 + 2 * p], columns[:, 24 + 2 * p : 25 + 2 * p]
        second = after[32 * p : 32 * p + 32] + prod[2 * p + 1]
        first = second + prod[2 * p]
        for k, share in ((0, first), (1, second)):
            q = 2 * p + k
            suffix = far + weighed(near, deep_w[q]) + (share - deep_o[q])
            g = step * dens[q] * suffix
            g = jnp.where(lane == 0, columns[:, q : q + 1], g)
            g = jnp.where(lane == 127, columns[:, 8 + q : 9 + q], g)
            grad[q] = g
            grads.append(g)
    fields = spread(grads, columns)
    odd, even_row = sides(to_row(0, fields, kernels, shard), to_row(2, fields, kernels, shard))
    odd_out[...] = odd
    even_out[...] = even_row


def finish(grad, columns, fields, kernels, mixing, out, own, halves):
    shard = lax.axis_index("rad")
    lane = lanes((32, 128))
    grads = [grad[q] for q in range(8)]
    acc = [fields[p] for p in range(8)]
    for q in range(8):
        block = mixing[q]
        for p in range(8):
            acc[p] = acc[p] + block[p : p + 1, :] * grads[q]
    for i in range(2):
        for j in range(2):
            pair = acc[4 * i + 2 * j : 4 * i + 2 * j + 2]
            half = pl.ds(j, 32, stride=2)
            for side in range(2):
                index = (lane >> 1) + 64 * side
                value = jnp.where((lane & 1) == 0, pick(pair[0], index), pick(pair[1], index))
                halves[side, half, :] = value
        for side in range(2):
            out[i, :, 128 * side : 128 * side + 128] = halves[side]
    own[...] = to_row(1, spread(grads, columns[...]), kernels, shard)


def call(body, ins, outs, flops, scratch=(), space=pltpu.VMEM):
    shapes = tuple(jax.ShapeDtypeStruct(s, d) for s, d in outs)
    size = sum(x.size * 4 for x in ins) + sum(x.size * 4 for x in shapes)
    return pl.pallas_call(
        body,
        out_shape=shapes,
        in_specs=[pl.BlockSpec(memory_space=space)] * len(ins),
        out_specs=tuple([VMEM] * len(shapes)),
        scratch_shapes=list(scratch),
        cost_estimate=pl.CostEstimate(flops=flops, bytes_accessed=size, transcendentals=0),
        compiler_params=pltpu.CompilerParams(vmem_limit_bytes=16 << 20),
    )(*ins)


def per_device(coarse, excite, kernels, mixing, star_bin, star_count, star_obs, star_isig):
    count = lax.axis_size("ang")
    pairs = [[], []]
    for i in range(count - 1):
        pairs[i % 2] += [(i, i + 1), (i + 1, i)]

    def exchange(odd, even):
        even = lax.ppermute(even, "ang", pairs[0])
        odd = lax.ppermute(odd, "ang", pairs[1])
        return odd, even

    own = coarse[0, 0]
    odd = lax.ppermute(own, "ang", pairs[1])
    even = lax.ppermute(own, "ang", pairs[0])
    block = ((8, 32, 128), F32)
    row = ((32, 128), F32)
    stars = [x.transpose(0, 2, 1) for x in (star_bin, star_obs, star_isig)]
    base, fields, hits_w, deep_w, deep_o, sums, mixing_here = call(
        prepare,
        [pltpu.with_memory_space_constraint(x, pltpu.HBM) for x in
         (own, excite[0], kernels, mixing, stars[0], star_count, stars[1], stars[2])],
        (block, block, block, block, block, row, ((8, 8, 128), F32)), 4_000_000,
        [pltpu.VMEM((128, 128), F32), pltpu.VMEM((2, 2, 64, 128), F32), pltpu.VMEM((32, 128), F32),
         pltpu.VMEM((9, 8, 128), F32), pltpu.VMEM((2, 16, 64), jnp.int32), pltpu.VMEM((2, 64), jnp.int32),
         pltpu.VMEM((2, 16, 64), F32), pltpu.VMEM((2, 16, 64), F32), pltpu.SemaphoreType.DMA((11,))],
        pltpu.HBM,
    )
    dens, prod, table = call(
        forward, (own, odd, even, base, kernels, hits_w, sums),
        (block, block, row), 6_000_000,
    )
    tables = lax.all_gather(table, "rad")
    grad, columns, odd, even = call(
        backward, (tables, dens, prod, kernels, deep_w, deep_o),
        (block, row, row, row), 8_000_000,
    )
    odd, even = exchange(odd, even)
    grad_excite, here = call(
        finish, (grad, columns, fields, kernels, mixing_here),
        (((2, 64, 256), F32), row), 4_000_000,
        [pltpu.VMEM((2, 64, 128), F32)],
    )
    grad_coarse = here + odd + even
    return grad_excite[None], grad_coarse[None, None]


def solution(mesh):
    in_specs = (
        P(None, "ang", None, "rad"),
        P(None, "ang", None, "rad"),
        P(),
        P(),
        P("ang", None, None),
        P("ang", None),
        P("ang", None, None),
        P("ang", None, None),
    )
    out_specs = (P(None, "ang", None, "rad"), P(None, "ang", None, "rad"))
    return jax.shard_map(
        per_device, mesh=mesh, in_specs=in_specs, out_specs=out_specs, check_vma=False
    )
```

```python
import jax
import jax.numpy as jnp
from jax import lax
from jax.experimental import pallas as pl
from jax.experimental.pallas import tpu as pltpu
from jax.sharding import PartitionSpec as P


F32 = jnp.float32
HI = lax.Precision.HIGHEST
VMEM = pl.BlockSpec(memory_space=pltpu.VMEM)


def lanes(shape):
    return lax.broadcasted_iota(jnp.int32, shape, 1)


def rows(shape):
    return lax.broadcasted_iota(jnp.int32, shape, 0)


def along(x, k, axis):
    if k == 0:
        return x
    n = x.shape[axis]
    at = lax.broadcasted_iota(jnp.int32, x.shape, axis)
    inside = at < n - k if k > 0 else at >= -k
    return jnp.where(inside, pltpu.roll(x, (-k) % n, axis), 0.0)


def pick(x, index):
    return jnp.take_along_axis(x, index, axis=1, mode="promise_in_bounds")


def split_pixels(ref, j):
    half = pl.ds(j, 32, stride=2)
    low, high = ref[0, half, :], ref[1, half, :]
    lane = lanes((32, 128))
    out = []
    for k in range(2):
        index = (2 * lane + k) & 127
        out.append(jnp.where(lane < 64, pick(low, index), pick(high, index)))
    return out


def pixels(p):
    return pl.ds(64 * (p // 2) + p % 2, 32, stride=2)


def taps(acc, row, weights):
    for w in range(3):
        moved = along(row, w - 1, 1)
        for v in range(3):
            window = along(moved, v - 1, 0)
            block = weights[3 * v + w]
            for q in range(8):
                acc[q] = acc[q] + block[q : q + 1, :] * window


def prepare(coarse_in, excite_in, kernels_in, mixing_in, bin_in, count_in, obs_in, isig_in,
            base, fields, stars, sums, mixing,
            turned, halves, coarse, kernels, star_bin, star_count, star_obs, star_isig, arrived):
    shard = lax.axis_index("rad")
    here = pl.ds(pl.multiple_of(shard * 128, 128), 128)
    moves = [(bin_in, star_bin), (count_in, star_count), (obs_in, star_obs), (isig_in, star_isig)]
    for i in range(2):
        for side in range(2):
            moves.append((excite_in.at[i, :, 128 * side : 128 * side + 128], halves.at[i, side]))
    moves += [(mixing_in.at[:, :, here], mixing), (coarse_in, coarse), (kernels_in.at[9:18, :, here], kernels)]
    moves = [pltpu.make_async_copy(a, b, arrived.at[n]) for n, (a, b) in enumerate(moves)]
    for move in moves:
        move.start()
    for move in moves[:4]:
        move.wait()

    def joined(x):
        return jnp.concatenate([x[0], x[1]], axis=1)

    count = jnp.concatenate([star_count[0:1, :], star_count[1:2, :]], axis=1)
    rel = joined(star_bin) - 256 * shard
    live = (rows((16, 128)) < count) & (rel >= 0) & (rel < 256)
    isig = joined(star_isig)
    w = jnp.where(live, isig * isig, 0.0)
    o = w * joined(star_obs)
    rel = jnp.where(live, rel, -1)
    hits = [[[], []], [[], []]]
    for tile in range(16):
        bin0 = 2 * (rows((8, 128)) + 8 * tile)
        bin1 = bin0 + 1
        total = [[jnp.zeros((8, 128), F32)] * 2 for _ in range(2)]
        for m in range(16):
            at = rel[m : m + 1, :]
            for k, bins in ((0, bin0), (1, bin1)):
                here_now = at == bins
                for f, value in ((0, w), (1, o)):
                    total[f][k] = total[f][k] + jnp.where(here_now, value[m : m + 1, :], 0.0)
        for f in range(2):
            for k in range(2):
                hits[f][k].append(total[f][k])
    hits = [[jnp.concatenate(hits[f][k], axis=0) for k in range(2)] for f in range(2)]
    pairs = jnp.concatenate([hits[f][0] + hits[f][1] for f in range(2)], axis=1)
    beyond = (lanes((128, 128)) > rows((128, 128))).astype(F32)
    after = jnp.dot(beyond, pairs, precision=HI, preferred_element_type=F32)
    ends = []
    for f in range(2):
        second = after[:, 128 * f : 128 * f + 128] + hits[f][1]
        first = second + hits[f][0]
        for k, value in ((0, first), (1, second)):
            stars[2 + 2 * f + k] = value.T
            ends.append((40 + 16 * f + k, value[0:1, :]))
            ends.append((48 + 16 * f + k, value[127:128, :]))
    for k in range(2):
        stars[k] = hits[0][k].T
    row = rows((8, 128))
    groups = [jnp.zeros((8, 128), F32)] * 16
    for at, value in ends:
        groups[at // 8] = jnp.where(row == at % 8, value, groups[at // 8])
    turned[...] = jnp.concatenate(groups, axis=0).T
    table = jnp.zeros((32, 128), F32)
    for p in range(4):
        table = table + pltpu.roll(turned[pixels(p), :], 2 * p, 1)
    sums[...] = table
    for move in moves[4:]:
        move.wait()
    parts = []
    for i in range(2):
        for j in range(2):
            parts += split_pixels(halves.at[i], j)
    for p in range(8):
        fields[p] = parts[p]
    acc = []
    for q in range(8):
        block = mixing[q]
        total = block[0:1, :] * parts[0]
        for p in range(1, 8):
            total = total + block[p : p + 1, :] * parts[p]
        acc.append(total)
    taps(acc, coarse[...], [kernels[t] for t in range(9)])
    for q in range(8):
        base[q] = acc[q]


def sides(odd, even):
    first = (lax.axis_index("ang") & 1) == 0
    return jnp.where(first, odd, even), jnp.where(first, even, odd)


def forward(coarse, odd, even, base, kernels, stars, sums, dens, prod, table):
    shard = lax.axis_index("rad")
    step = 1.0 / 1024
    acc = [base[q] for q in range(8)]
    low, high = sides(odd[...], even[...])
    here = pl.ds(pl.multiple_of(shard * 128, 128), 128)
    taps(acc, low, [kernels[t, :, here] for t in range(9)])
    taps(acc, high, [kernels[t, :, here] for t in range(18, 27)])
    lane = lanes((32, 128))
    out = sums[...]
    for q in range(8):
        out = jnp.where(lane == q, acc[q][:, 0:1], out)
        out = jnp.where(lane == 8 + q, acc[q][:, 127:128], out)
    for u, value in enumerate((low, coarse[...], high)):
        out = jnp.where(lane == 32 + u, value[:, 0:1], out)
        out = jnp.where(lane == 35 + u, value[:, 127:128], out)
    inner = (lane > 0) & (lane < 127)
    density = []
    for q in range(8):
        d = jnp.exp(acc[q])
        dens[q] = d
        density.append(jnp.where(inner, d, 0.0))
    pairs = jnp.concatenate([density[2 * p] + density[2 * p + 1] for p in range(4)], axis=0)
    strict = (rows((128, 128)) < lanes((128, 128))).astype(F32)
    before = jnp.dot(pairs, strict, precision=HI, preferred_element_type=F32)
    for p in range(4):
        first = before[32 * p : 32 * p + 32] + density[2 * p]
        second = first + density[2 * p + 1]
        first = weighed(step * first, stars[0, pixels(p), :])
        total = second[:, 127:128]
        second = weighed(step * second, stars[1, pixels(p), :])
        prod[2 * p] = first
        prod[2 * p + 1] = second
        share = jnp.sum(first + second, axis=1, keepdims=True)
        for k in range(2):
            out = jnp.where(lane == 16 + 2 * p + k, total, out)
            out = jnp.where(lane == 24 + 2 * p + k, share, out)
    table[...] = out


def weighed(x, w):
    return jnp.where(w != 0.0, x * w, 0.0)


def swap(x):
    even = (rows(x.shape) & 1) == 0
    return jnp.where(even, pltpu.roll(x, x.shape[0] - 1, 0), pltpu.roll(x, 1, 0))


def spread(grad, columns):
    lane = lanes((32, 128))
    plus, minus = [], []
    for q in range(8):
        plus.append(jnp.where(lane == 127, columns[:, 32 + q : 33 + q], grad[q]))
        minus.append(jnp.where(lane == 0, columns[:, 40 + q : 41 + q], grad[q]))
    return minus, grad, plus


def to_row(u, fields, kernels, shard):
    at = pl.ds(pl.multiple_of(shard * 128, 128), 128)
    prev = pl.ds(pl.multiple_of(jnp.maximum(shard - 1, 0) * 128, 128), 128)
    after = pl.ds(pl.multiple_of(jnp.minimum(shard + 1, 3) * 128, 128), 128)
    lane = lanes((8, 128))
    total = None
    for w, field in enumerate(fields):
        part = None
        for v in range(3):
            t = 9 * u + 3 * v + w
            block = kernels[t, :, at]
            if w == 0:
                block = jnp.where(lane == 0, kernels[t, :, after], block)
            if w == 2:
                block = jnp.where(lane == 127, kernels[t, :, prev], block)
            piece = block[0:1, :] * field[0]
            for q in range(1, 8):
                piece = piece + block[q : q + 1, :] * field[q]
            piece = along(piece, 1 - v, 0)
            part = piece if part is None else part + piece
        if w != 1:
            part = pltpu.roll(part, (w - 1) % 128, 1)
        total = part if total is None else total + part
    return total


def backward(own, by1, by2, by3, dens, prod, kernels, stars, grad, edges_out, odd_out, even_out):
    shard = lax.axis_index("rad")
    step = 1.0 / 1024
    even = (rows((8, 128)) & 1) == 0
    pairs = jnp.concatenate([prod[2 * p] + prod[2 * p + 1] for p in range(4)], axis=0)
    beyond = (rows((128, 128)) > lanes((128, 128))).astype(F32)
    after = jnp.dot(pairs, beyond, precision=HI, preferred_element_type=F32)
    held = [own[...], by1[...], by2[...], by3[...]]
    groups = []
    for s in range(4):
        table = held[0]
        for k in range(1, 4):
            table = jnp.where(shard == (s ^ k), held[k], table)
        full = jnp.concatenate([table, jnp.zeros((96, 128), F32)], axis=0).T
        groups.append([full[8 * g : 8 * g + 8] for g in range(9)])
    edges = []
    for s in range(4):
        e = groups[s][4]
        edges.append([along(e, v - 1, 1) for v in range(3)])
    d_low, d_high, totals, shares, whole, tails = [], [], [], [], [], []
    for s in range(4):
        f_low, f_high, t, c, _, w_low, w_high, o_low, _ = groups[s]
        for u in range(3):
            for v in range(3):
                if s > 0:
                    weight = kernels[9 * u + 3 * v, :, 128 * s : 128 * s + 128][:, 0:1]
                    f_low = f_low + weight * edges[s - 1][v][3 + u : 4 + u, :]
                if s < 3:
                    weight = kernels[9 * u + 3 * v + 2, :, 128 * s : 128 * s + 128][:, 127:128]
                    f_high = f_high + weight * edges[s + 1][v][u : u + 1, :]
        a, b = jnp.exp(f_low), jnp.exp(f_high)
        d_low.append(a)
        d_high.append(b)
        both = a + b
        totals.append(t + both + swap(both))
        tail = step * b * w_high
        tail = tail + swap(tail)
        tails.append(tail)
        head = step * a * w_low
        o_all = jnp.where(even, o_low, swap(o_low))
        shares.append(c - o_all + head + swap(head) + tail)
        whole.append(jnp.where(even, w_low, swap(w_low)))
    zero = jnp.zeros((8, 128), F32)
    nearer = [zero]
    for s in range(3):
        nearer.append(nearer[s] + totals[s])
    nearer = [step * x for x in nearer]
    sums = [shares[s] + weighed(nearer[s], whole[s]) for s in range(4)]
    farther = [zero]
    for s in (3, 2, 1):
        farther.insert(0, farther[0] + sums[s])

    def low_edge(s):
        w, o = groups[s][5], groups[s][7]
        first = weighed(nearer[s] + step * swap(d_low[s]), swap(w) - w) - (swap(o) - o)
        suffix = sums[s] - jnp.where(even, 0.0, first)
        return d_low[s] * step * (farther[s] + suffix)

    def high_edge(s):
        w, o = groups[s][6], groups[s][8]
        last = step * swap(d_high[s]) * (w - swap(w))
        suffix = weighed(nearer[s] + step * totals[s], w) - o - jnp.where(even, last, 0.0)
        return d_high[s] * step * (farther[s] + suffix)

    def mine(values):
        out = values[0]
        for s in range(1, 4):
            out = jnp.where(shard == s, values[s], out)
        return out

    lows = [low_edge(s) for s in range(4)]
    highs = [high_edge(s) for s in range(4)]
    columns = [mine(lows), mine(highs),
               mine([nearer[s] + step * (d_low[s] + swap(d_low[s])) for s in range(4)]),
               mine([farther[s] + tails[s] for s in range(4)]),
               mine([zero] + highs[:3]), mine(lows[1:] + [zero])]
    columns = jnp.concatenate(columns + [jnp.zeros((80, 128), F32)], axis=0).T[0:32]
    edges_out[...] = columns
    lane = lanes((32, 128))
    grads = []
    for p in range(4):
        near, far = columns[:, 16 + 2 * p : 17 + 2 * p], columns[:, 24 + 2 * p : 25 + 2 * p]
        second = after[32 * p : 32 * p + 32] + prod[2 * p + 1]
        first = second + prod[2 * p]
        for k, share in ((0, first), (1, second)):
            q = 2 * p + k
            suffix = far + weighed(near, stars[2 + k, pixels(p), :]) + (share - stars[4 + k, pixels(p), :])
            g = step * dens[q] * suffix
            g = jnp.where(lane == 0, columns[:, q : q + 1], g)
            g = jnp.where(lane == 127, columns[:, 8 + q : 9 + q], g)
            grad[q] = g
            grads.append(g)
    fields = spread(grads, columns)
    odd, even_row = sides(to_row(0, fields, kernels, shard), to_row(2, fields, kernels, shard))
    odd_out[...] = odd
    even_out[...] = even_row


def finish(grad, columns, fields, kernels, mixing, even, odd, out, own, halves):
    shard = lax.axis_index("rad")
    lane = lanes((32, 128))
    grads = [grad[q] for q in range(8)]
    acc = [fields[p] for p in range(8)]
    for q in range(8):
        block = mixing[q]
        for p in range(8):
            acc[p] = acc[p] + block[p : p + 1, :] * grads[q]
    for i in range(2):
        for j in range(2):
            pair = acc[4 * i + 2 * j : 4 * i + 2 * j + 2]
            half = pl.ds(j, 32, stride=2)
            for side in range(2):
                index = (lane >> 1) + 64 * side
                value = jnp.where((lane & 1) == 0, pick(pair[0], index), pick(pair[1], index))
                halves[side, half, :] = value
        for side in range(2):
            out[i, :, 128 * side : 128 * side + 128] = halves[side]
    place = lax.axis_index("ang")
    other = jnp.where((place & 1) == 0, odd[0:32], odd[32:64])
    met = (place > 0) & (place < lax.axis_size("ang") - 1)
    total = to_row(1, spread(grads, columns[...]), kernels, shard) + even[...]
    own[...] = total + jnp.where(met, other, 0.0)


def call(body, ins, outs, flops, scratch=(), space=pltpu.VMEM):
    shapes = tuple(jax.ShapeDtypeStruct(s, d) for s, d in outs)
    size = sum(x.size * 4 for x in ins) + sum(x.size * 4 for x in shapes)
    return pl.pallas_call(
        body,
        out_shape=shapes,
        in_specs=[pl.BlockSpec(memory_space=space)] * len(ins),
        out_specs=tuple([VMEM] * len(shapes)),
        scratch_shapes=list(scratch),
        cost_estimate=pl.CostEstimate(flops=flops, bytes_accessed=size, transcendentals=0),
        compiler_params=pltpu.CompilerParams(vmem_limit_bytes=16 << 20),
    )(*ins)


def per_device(coarse, excite, kernels, mixing, star_bin, star_count, star_obs, star_isig):
    count = lax.axis_size("ang")
    pairs = [[], []]
    for i in range(count - 1):
        pairs[i % 2] += [(i, i + 1), (i + 1, i)]

    own = coarse[0, 0]
    odd = lax.ppermute(own, "ang", pairs[1])
    even = lax.ppermute(own, "ang", pairs[0])
    block = ((8, 32, 128), F32)
    row = ((32, 128), F32)
    stars = [x.transpose(0, 2, 1) for x in (star_bin, star_obs, star_isig)]
    base, fields, stars, sums, mixing_here = call(
        prepare,
        [pltpu.with_memory_space_constraint(x, pltpu.HBM) for x in
         (own, excite[0], kernels, mixing, stars[0], star_count, stars[1], stars[2])],
        (block, block, ((6, 128, 128), F32), row, ((8, 8, 128), F32)), 4_000_000,
        [pltpu.VMEM((128, 128), F32), pltpu.VMEM((2, 2, 64, 128), F32), pltpu.VMEM((32, 128), F32),
         pltpu.VMEM((9, 8, 128), F32), pltpu.VMEM((2, 16, 64), jnp.int32), pltpu.VMEM((2, 64), jnp.int32),
         pltpu.VMEM((2, 16, 64), F32), pltpu.VMEM((2, 16, 64), F32), pltpu.SemaphoreType.DMA((11,))],
        pltpu.HBM,
    )
    dens, prod, table = call(
        forward, (own, odd, even, base, kernels, stars, sums),
        (block, block, row), 6_000_000,
    )
    others = [lax.ppermute(table, "rad", [(i, i ^ k) for i in range(4)]) for k in (1, 2, 3)]
    grad, columns, odd, even = call(
        backward, (table, *others, dens, prod, kernels, stars),
        (block, row, row, row), 8_000_000,
    )
    even = lax.ppermute(even, "ang", pairs[0])
    groups = [[i, (i + 1) % count] for i in range(1, count, 2)]
    odd = lax.all_gather(odd, "ang", axis_index_groups=groups, tiled=True)
    grad_excite, grad_coarse = call(
        finish, (grad, columns, fields, kernels, mixing_here, even, odd),
        (((2, 64, 256), F32), row), 4_000_000,
        [pltpu.VMEM((2, 64, 128), F32)],
    )
    return grad_excite[None], grad_coarse[None, None]


def solution(mesh):
    in_specs = (
        P(None, "ang", None, "rad"),
        P(None, "ang", None, "rad"),
        P(),
        P(),
        P("ang", None, None),
        P("ang", None),
        P("ang", None, None),
        P("ang", None, None),
    )
    out_specs = (P(None, "ang", None, "rad"), P(None, "ang", None, "rad"))
    return jax.shard_map(
        per_device, mesh=mesh, in_specs=in_specs, out_specs=out_specs, check_vma=False
    )
```

```python
import jax
import jax.numpy as jnp
from jax import lax
from jax.experimental import pallas as pl
from jax.experimental.pallas import tpu as pltpu
from jax.sharding import PartitionSpec as P


F32 = jnp.float32
HI = lax.Precision.HIGHEST
VMEM = pl.BlockSpec(memory_space=pltpu.VMEM)


def lanes(shape):
    return lax.broadcasted_iota(jnp.int32, shape, 1)


def rows(shape):
    return lax.broadcasted_iota(jnp.int32, shape, 0)


def along(x, k, axis):
    if k == 0:
        return x
    n = x.shape[axis]
    at = lax.broadcasted_iota(jnp.int32, x.shape, axis)
    inside = at < n - k if k > 0 else at >= -k
    return jnp.where(inside, pltpu.roll(x, (-k) % n, axis), 0.0)


def pick(x, index):
    return jnp.take_along_axis(x, index, axis=1, mode="promise_in_bounds")


def split_pixels(ref, j):
    half = pl.ds(j, 32, stride=2)
    low, high = ref[0, half, :], ref[1, half, :]
    lane = lanes((32, 128))
    out = []
    for k in range(2):
        index = (2 * lane + k) & 127
        out.append(jnp.where(lane < 64, pick(low, index), pick(high, index)))
    return out


def pixels(p):
    return pl.ds(64 * (p // 2) + p % 2, 32, stride=2)


def taps(acc, row, weights):
    for w in range(3):
        moved = along(row, w - 1, 1)
        for v in range(3):
            window = along(moved, v - 1, 0)
            block = weights[3 * v + w]
            for q in range(8):
                acc[q] = acc[q] + block[q : q + 1, :] * window


def prepare(coarse_in, excite_in, kernels_in, mixing_in, bin_in, count_in, obs_in, isig_in,
            base, fields, stars, sums, mixing,
            turned, halves, coarse, kernels, star_bin, star_count, star_obs, star_isig, arrived):
    shard = lax.axis_index("rad")
    here = pl.ds(pl.multiple_of(shard * 128, 128), 128)
    moves = [(bin_in, star_bin), (count_in, star_count), (obs_in, star_obs), (isig_in, star_isig)]
    for i in range(2):
        for side in range(2):
            moves.append((excite_in.at[i, :, 128 * side : 128 * side + 128], halves.at[i, side]))
    moves += [(mixing_in.at[:, :, here], mixing), (coarse_in, coarse), (kernels_in.at[9:18, :, here], kernels)]
    moves = [pltpu.make_async_copy(a, b, arrived.at[n]) for n, (a, b) in enumerate(moves)]
    for move in moves:
        move.start()
    for move in moves[:4]:
        move.wait()

    def joined(x):
        return jnp.concatenate([x[0], x[1]], axis=1)

    count = jnp.concatenate([star_count[0:1, :], star_count[1:2, :]], axis=1)
    rel = joined(star_bin) - 256 * shard
    live = (rows((16, 128)) < count) & (rel >= 0) & (rel < 256)
    isig = joined(star_isig)
    w = jnp.where(live, isig * isig, 0.0)
    o = w * joined(star_obs)
    rel = jnp.where(live, rel, -1)
    hits = [[[], []], [[], []]]
    for tile in range(16):
        bin0 = 2 * (rows((8, 128)) + 8 * tile)
        bin1 = bin0 + 1
        total = [[jnp.zeros((8, 128), F32)] * 2 for _ in range(2)]
        for m in range(16):
            at = rel[m : m + 1, :]
            for k, bins in ((0, bin0), (1, bin1)):
                here_now = at == bins
                for f, value in ((0, w), (1, o)):
                    total[f][k] = total[f][k] + jnp.where(here_now, value[m : m + 1, :], 0.0)
        for f in range(2):
            for k in range(2):
                hits[f][k].append(total[f][k])
    hits = [[jnp.concatenate(hits[f][k], axis=0) for k in range(2)] for f in range(2)]
    pairs = jnp.concatenate([hits[f][0] + hits[f][1] for f in range(2)], axis=1)
    beyond = (lanes((128, 128)) > rows((128, 128))).astype(F32)
    after = jnp.dot(beyond, pairs, precision=HI, preferred_element_type=F32)
    ends = []
    for f in range(2):
        second = after[:, 128 * f : 128 * f + 128] + hits[f][1]
        first = second + hits[f][0]
        for k, value in ((0, first), (1, second)):
            stars[2 + 2 * f + k] = value.T
            ends.append((40 + 16 * f + k, value[0:1, :]))
            ends.append((48 + 16 * f + k, value[127:128, :]))
    for k in range(2):
        stars[k] = hits[0][k].T
    row = rows((8, 128))
    groups = [jnp.zeros((8, 128), F32)] * 16
    for at, value in ends:
        groups[at // 8] = jnp.where(row == at % 8, value, groups[at // 8])
    turned[...] = jnp.concatenate(groups, axis=0).T
    table = jnp.zeros((32, 128), F32)
    for p in range(4):
        table = table + pltpu.roll(turned[pixels(p), :], 2 * p, 1)
    sums[...] = table
    for move in moves[4:]:
        move.wait()
    parts = []
    for i in range(2):
        for j in range(2):
            parts += split_pixels(halves.at[i], j)
    for p in range(8):
        fields[p] = parts[p]
    acc = []
    for q in range(8):
        block = mixing[q]
        total = block[0:1, :] * parts[0]
        for p in range(1, 8):
            total = total + block[p : p + 1, :] * parts[p]
        acc.append(total)
    taps(acc, coarse[...], [kernels[t] for t in range(9)])
    for q in range(8):
        base[q] = acc[q]


def sides(odd, even):
    first = (lax.axis_index("ang") & 1) == 0
    return jnp.where(first, odd, even), jnp.where(first, even, odd)


def forward(coarse, odd, even, base, kernels, stars, sums, dens, prod, table):
    shard = lax.axis_index("rad")
    step = 1.0 / 1024
    acc = [base[q] for q in range(8)]
    low, high = sides(odd[...], even[...])
    here = pl.ds(pl.multiple_of(shard * 128, 128), 128)
    taps(acc, low, [kernels[t, :, here] for t in range(9)])
    taps(acc, high, [kernels[t, :, here] for t in range(18, 27)])
    lane = lanes((32, 128))
    out = sums[...]
    for q in range(8):
        out = jnp.where(lane == q, acc[q][:, 0:1], out)
        out = jnp.where(lane == 8 + q, acc[q][:, 127:128], out)
    for u, value in enumerate((low, coarse[...], high)):
        out = jnp.where(lane == 32 + u, value[:, 0:1], out)
        out = jnp.where(lane == 35 + u, value[:, 127:128], out)
    inner = (lane > 0) & (lane < 127)
    density = []
    for q in range(8):
        d = jnp.exp(acc[q])
        dens[q] = d
        density.append(jnp.where(inner, d, 0.0))
    pairs = jnp.concatenate([density[2 * p] + density[2 * p + 1] for p in range(4)], axis=0)
    strict = (rows((128, 128)) < lanes((128, 128))).astype(F32)
    before = jnp.dot(pairs, strict, precision=HI, preferred_element_type=F32)
    for p in range(4):
        first = before[32 * p : 32 * p + 32] + density[2 * p]
        second = first + density[2 * p + 1]
        first = weighed(step * first, stars[0, pixels(p), :])
        total = second[:, 127:128]
        second = weighed(step * second, stars[1, pixels(p), :])
        prod[2 * p] = first
        prod[2 * p + 1] = second
        share = jnp.sum(first + second, axis=1, keepdims=True)
        for k in range(2):
            out = jnp.where(lane == 16 + 2 * p + k, total, out)
            out = jnp.where(lane == 24 + 2 * p + k, share, out)
    table[...] = out


def weighed(x, w):
    return jnp.where(w != 0.0, x * w, 0.0)


def swap(x):
    even = (rows(x.shape) & 1) == 0
    return jnp.where(even, pltpu.roll(x, x.shape[0] - 1, 0), pltpu.roll(x, 1, 0))


def spread(grad, columns):
    lane = lanes((32, 128))
    plus, minus = [], []
    for q in range(8):
        plus.append(jnp.where(lane == 127, columns[:, 32 + q : 33 + q], grad[q]))
        minus.append(jnp.where(lane == 0, columns[:, 40 + q : 41 + q], grad[q]))
    return minus, grad, plus


def to_row(u, fields, kernels, shard):
    at = pl.ds(pl.multiple_of(shard * 128, 128), 128)
    prev = pl.ds(pl.multiple_of(jnp.maximum(shard - 1, 0) * 128, 128), 128)
    after = pl.ds(pl.multiple_of(jnp.minimum(shard + 1, 3) * 128, 128), 128)
    lane = lanes((8, 128))
    total = None
    for w, field in enumerate(fields):
        part = None
        for v in range(3):
            t = 9 * u + 3 * v + w
            block = kernels[t, :, at]
            if w == 0:
                block = jnp.where(lane == 0, kernels[t, :, after], block)
            if w == 2:
                block = jnp.where(lane == 127, kernels[t, :, prev], block)
            piece = block[0:1, :] * field[0]
            for q in range(1, 8):
                piece = piece + block[q : q + 1, :] * field[q]
            piece = along(piece, 1 - v, 0)
            part = piece if part is None else part + piece
        if w != 1:
            part = pltpu.roll(part, (w - 1) % 128, 1)
        total = part if total is None else total + part
    return total


def middle(prod, stars, kernels, share, weights):
    pairs = jnp.concatenate([prod[2 * p] + prod[2 * p + 1] for p in range(4)], axis=0)
    beyond = (rows((128, 128)) > lanes((128, 128))).astype(F32)
    after = jnp.dot(pairs, beyond, precision=HI, preferred_element_type=F32)
    for p in range(4):
        second = after[32 * p : 32 * p + 32] + prod[2 * p + 1]
        first = second + prod[2 * p]
        for k, value in ((0, first), (1, second)):
            share[2 * p + k] = value - stars[4 + k, pixels(p), :]
    for s in range(4):
        for n in range(9):
            for side in range(2):
                block = kernels[3 * n + 2 * side, :, 128 * s : 128 * s + 128]
                weights[s, side, n] = jnp.broadcast_to(block[:, 127 * side : 127 * side + 1], (8, 128))


def backward(own, by1, by2, by3, dens, share, weights, kernels, stars, grad, edges_out, odd_out, even_out):
    shard = lax.axis_index("rad")
    step = 1.0 / 1024
    even = (rows((8, 128)) & 1) == 0
    held = [own[...], by1[...], by2[...], by3[...]]
    groups = []
    for s in range(4):
        table = held[0]
        for k in range(1, 4):
            table = jnp.where(shard == (s ^ k), held[k], table)
        full = jnp.concatenate([table, jnp.zeros((96, 128), F32)], axis=0).T
        groups.append([full[8 * g : 8 * g + 8] for g in range(9)])
    edges = []
    for s in range(4):
        e = groups[s][4]
        edges.append([along(e, v - 1, 1) for v in range(3)])
    d_low, d_high, totals, shares, whole, tails = [], [], [], [], [], []
    for s in range(4):
        f_low, f_high, t, c, _, w_low, w_high, o_low, _ = groups[s]
        for u in range(3):
            for v in range(3):
                if s > 0:
                    f_low = f_low + weights[s, 0, 3 * u + v] * edges[s - 1][v][3 + u : 4 + u, :]
                if s < 3:
                    f_high = f_high + weights[s, 1, 3 * u + v] * edges[s + 1][v][u : u + 1, :]
        a, b = jnp.exp(f_low), jnp.exp(f_high)
        d_low.append(a)
        d_high.append(b)
        both = a + b
        totals.append(t + both + swap(both))
        tail = step * b * w_high
        tail = tail + swap(tail)
        tails.append(tail)
        head = step * a * w_low
        o_all = jnp.where(even, o_low, swap(o_low))
        shares.append(c - o_all + head + swap(head) + tail)
        whole.append(jnp.where(even, w_low, swap(w_low)))
    zero = jnp.zeros((8, 128), F32)
    nearer = [zero]
    for s in range(3):
        nearer.append(nearer[s] + totals[s])
    nearer = [step * x for x in nearer]
    sums = [shares[s] + weighed(nearer[s], whole[s]) for s in range(4)]
    farther = [zero]
    for s in (3, 2, 1):
        farther.insert(0, farther[0] + sums[s])

    def low_edge(s):
        w, o = groups[s][5], groups[s][7]
        first = weighed(nearer[s] + step * swap(d_low[s]), swap(w) - w) - (swap(o) - o)
        suffix = sums[s] - jnp.where(even, 0.0, first)
        return d_low[s] * step * (farther[s] + suffix)

    def high_edge(s):
        w, o = groups[s][6], groups[s][8]
        last = step * swap(d_high[s]) * (w - swap(w))
        suffix = weighed(nearer[s] + step * totals[s], w) - o - jnp.where(even, last, 0.0)
        return d_high[s] * step * (farther[s] + suffix)

    def mine(values):
        out = values[0]
        for s in range(1, 4):
            out = jnp.where(shard == s, values[s], out)
        return out

    lows = [low_edge(s) for s in range(4)]
    highs = [high_edge(s) for s in range(4)]
    columns = [mine(lows), mine(highs),
               mine([nearer[s] + step * (d_low[s] + swap(d_low[s])) for s in range(4)]),
               mine([farther[s] + tails[s] for s in range(4)]),
               mine([zero] + highs[:3]), mine(lows[1:] + [zero])]
    columns = jnp.concatenate(columns + [jnp.zeros((80, 128), F32)], axis=0).T[0:32]
    edges_out[...] = columns
    lane = lanes((32, 128))
    grads = []
    for p in range(4):
        near, far = columns[:, 16 + 2 * p : 17 + 2 * p], columns[:, 24 + 2 * p : 25 + 2 * p]
        for k in range(2):
            q = 2 * p + k
            suffix = far + weighed(near, stars[2 + k, pixels(p), :]) + share[q]
            g = step * dens[q] * suffix
            g = jnp.where(lane == 0, columns[:, q : q + 1], g)
            g = jnp.where(lane == 127, columns[:, 8 + q : 9 + q], g)
            grad[q] = g
            grads.append(g)
    fields = spread(grads, columns)
    odd, even_row = sides(to_row(0, fields, kernels, shard), to_row(2, fields, kernels, shard))
    odd_out[...] = odd
    even_out[...] = even_row


def finish(grad, columns, fields, kernels, mixing, even, odd, out, own, halves):
    shard = lax.axis_index("rad")
    lane = lanes((32, 128))
    grads = [grad[q] for q in range(8)]
    acc = [fields[p] for p in range(8)]
    for q in range(8):
        block = mixing[q]
        for p in range(8):
            acc[p] = acc[p] + block[p : p + 1, :] * grads[q]
    for i in range(2):
        for j in range(2):
            pair = acc[4 * i + 2 * j : 4 * i + 2 * j + 2]
            half = pl.ds(j, 32, stride=2)
            for side in range(2):
                index = (lane >> 1) + 64 * side
                value = jnp.where((lane & 1) == 0, pick(pair[0], index), pick(pair[1], index))
                halves[side, half, :] = value
        for side in range(2):
            out[i, :, 128 * side : 128 * side + 128] = halves[side]
    place = lax.axis_index("ang")
    other = jnp.where((place & 1) == 0, odd[0:32], odd[32:64])
    met = (place > 0) & (place < lax.axis_size("ang") - 1)
    total = to_row(1, spread(grads, columns[...]), kernels, shard) + even[...]
    own[...] = total + jnp.where(met, other, 0.0)


def call(body, ins, outs, flops, scratch=(), space=pltpu.VMEM):
    shapes = tuple(jax.ShapeDtypeStruct(s, d) for s, d in outs)
    size = sum(x.size * 4 for x in ins) + sum(x.size * 4 for x in shapes)
    return pl.pallas_call(
        body,
        out_shape=shapes,
        in_specs=[pl.BlockSpec(memory_space=space)] * len(ins),
        out_specs=tuple([VMEM] * len(shapes)),
        scratch_shapes=list(scratch),
        cost_estimate=pl.CostEstimate(flops=flops, bytes_accessed=size, transcendentals=0),
        compiler_params=pltpu.CompilerParams(vmem_limit_bytes=16 << 20),
    )(*ins)


def per_device(coarse, excite, kernels, mixing, star_bin, star_count, star_obs, star_isig):
    count = lax.axis_size("ang")
    pairs = [[], []]
    for i in range(count - 1):
        pairs[i % 2] += [(i, i + 1), (i + 1, i)]

    own = coarse[0, 0]
    odd = lax.ppermute(own, "ang", pairs[1])
    even = lax.ppermute(own, "ang", pairs[0])
    block = ((8, 32, 128), F32)
    row = ((32, 128), F32)
    stars = [x.transpose(0, 2, 1) for x in (star_bin, star_obs, star_isig)]
    base, fields, stars, sums, mixing_here = call(
        prepare,
        [pltpu.with_memory_space_constraint(x, pltpu.HBM) for x in
         (own, excite[0], kernels, mixing, stars[0], star_count, stars[1], stars[2])],
        (block, block, ((6, 128, 128), F32), row, ((8, 8, 128), F32)), 4_000_000,
        [pltpu.VMEM((128, 128), F32), pltpu.VMEM((2, 2, 64, 128), F32), pltpu.VMEM((32, 128), F32),
         pltpu.VMEM((9, 8, 128), F32), pltpu.VMEM((2, 16, 64), jnp.int32), pltpu.VMEM((2, 64), jnp.int32),
         pltpu.VMEM((2, 16, 64), F32), pltpu.VMEM((2, 16, 64), F32), pltpu.SemaphoreType.DMA((11,))],
        pltpu.HBM,
    )
    dens, prod, table = call(
        forward, (own, odd, even, base, kernels, stars, sums),
        (block, block, row), 6_000_000,
    )
    others = [lax.ppermute(table, "rad", [(i, i ^ k) for i in range(4)]) for k in (1, 2, 3)]
    share, weights = call(
        middle, (prod, stars, kernels), (block, ((4, 2, 9, 8, 128), F32)), 1_000_000,
    )
    grad, columns, odd, even = call(
        backward, (table, *others, dens, share, weights, kernels, stars),
        (block, row, row, row), 8_000_000,
    )
    even = lax.ppermute(even, "ang", pairs[0])
    near = lax.axis_size("rad")
    groups = [[i * near + r, (i + 1) * near + r] for i in range(1, count - 1, 2) for r in range(near)]
    groups += [[i * near + r, i * near + r + 1] for i in (0, count - 1) for r in range(0, near, 2)]
    odd = lax.all_gather(odd, ("ang", "rad"), axis_index_groups=groups, tiled=True)
    grad_excite, grad_coarse = call(
        finish, (grad, columns, fields, kernels, mixing_here, even, odd),
        (((2, 64, 256), F32), row), 4_000_000,
        [pltpu.VMEM((2, 64, 128), F32)],
    )
    return grad_excite[None], grad_coarse[None, None]


def solution(mesh):
    in_specs = (
        P(None, "ang", None, "rad"),
        P(None, "ang", None, "rad"),
        P(),
        P(),
        P("ang", None, None),
        P("ang", None),
        P("ang", None, None),
        P("ang", None, None),
    )
    out_specs = (P(None, "ang", None, "rad"), P(None, "ang", None, "rad"))
    return jax.shard_map(
        per_device, mesh=mesh, in_specs=in_specs, out_specs=out_specs, check_vma=False
    )
```

```python
import jax
import jax.numpy as jnp
from jax import lax
from jax.experimental import pallas as pl
from jax.experimental.pallas import tpu as pltpu
from jax.sharding import PartitionSpec as P


F32 = jnp.float32
HI = lax.Precision.HIGHEST
VMEM = pl.BlockSpec(memory_space=pltpu.VMEM)


def lanes(shape):
    return lax.broadcasted_iota(jnp.int32, shape, 1)


def rows(shape):
    return lax.broadcasted_iota(jnp.int32, shape, 0)


def along(x, k, axis):
    if k == 0:
        return x
    n = x.shape[axis]
    at = lax.broadcasted_iota(jnp.int32, x.shape, axis)
    inside = at < n - k if k > 0 else at >= -k
    return jnp.where(inside, pltpu.roll(x, (-k) % n, axis), 0.0)


def pick(x, index):
    return jnp.take_along_axis(x, index, axis=1, mode="promise_in_bounds")


def split_pixels(ref, j):
    half = pl.ds(j, 32, stride=2)
    low, high = ref[0, half, :], ref[1, half, :]
    lane = lanes((32, 128))
    out = []
    for k in range(2):
        index = (2 * lane + k) & 127
        out.append(jnp.where(lane < 64, pick(low, index), pick(high, index)))
    return out


def pixels(p):
    return pl.ds(64 * (p // 2) + p % 2, 32, stride=2)


def taps(acc, row, weights):
    for w in range(3):
        moved = along(row, w - 1, 1)
        for v in range(3):
            window = along(moved, v - 1, 0)
            block = weights[3 * v + w]
            for q in range(8):
                acc[q] = acc[q] + block[q : q + 1, :] * window


def prepare(coarse_in, excite_in, kernels_in, mixing_in, bin_in, count_in, obs_in, isig_in,
            base, fields, stars, sums, mixing,
            turned, halves, coarse, kernels, star_bin, star_count, star_obs, star_isig, arrived):
    shard = lax.axis_index("rad")
    here = pl.ds(pl.multiple_of(shard * 128, 128), 128)
    moves = [(bin_in, star_bin), (count_in, star_count), (obs_in, star_obs), (isig_in, star_isig)]
    for i in range(2):
        for side in range(2):
            moves.append((excite_in.at[i, :, 128 * side : 128 * side + 128], halves.at[i, side]))
    moves += [(mixing_in.at[:, :, here], mixing), (coarse_in, coarse), (kernels_in.at[9:18, :, here], kernels)]
    moves = [pltpu.make_async_copy(a, b, arrived.at[n]) for n, (a, b) in enumerate(moves)]
    for move in moves:
        move.start()
    for move in moves[:4]:
        move.wait()

    def joined(x):
        return jnp.concatenate([x[0], x[1]], axis=1)

    count = jnp.concatenate([star_count[0:1, :], star_count[1:2, :]], axis=1)
    rel = joined(star_bin) - 256 * shard
    live = (rows((16, 128)) < count) & (rel >= 0) & (rel < 256)
    isig = joined(star_isig)
    w = jnp.where(live, isig * isig, 0.0)
    o = w * joined(star_obs)
    rel = jnp.where(live, rel, -1)
    hits = [[[], []], [[], []]]
    for tile in range(16):
        bin0 = 2 * (rows((8, 128)) + 8 * tile)
        bin1 = bin0 + 1
        total = [[jnp.zeros((8, 128), F32)] * 2 for _ in range(2)]
        for m in range(16):
            at = rel[m : m + 1, :]
            for k, bins in ((0, bin0), (1, bin1)):
                here_now = at == bins
                for f, value in ((0, w), (1, o)):
                    total[f][k] = total[f][k] + jnp.where(here_now, value[m : m + 1, :], 0.0)
        for f in range(2):
            for k in range(2):
                hits[f][k].append(total[f][k])
    hits = [[jnp.concatenate(hits[f][k], axis=0) for k in range(2)] for f in range(2)]
    pairs = jnp.concatenate([hits[f][0] + hits[f][1] for f in range(2)], axis=1)
    beyond = (lanes((128, 128)) > rows((128, 128))).astype(F32)
    after = jnp.dot(beyond, pairs, precision=HI, preferred_element_type=F32)
    ends = []
    for f in range(2):
        second = after[:, 128 * f : 128 * f + 128] + hits[f][1]
        first = second + hits[f][0]
        for k, value in ((0, first), (1, second)):
            stars[2 + 2 * f + k] = value.T
            ends.append((40 + 16 * f + k, value[0:1, :]))
            ends.append((48 + 16 * f + k, value[127:128, :]))
    for k in range(2):
        stars[k] = hits[0][k].T
    row = rows((8, 128))
    groups = [jnp.zeros((8, 128), F32)] * 16
    for at, value in ends:
        groups[at // 8] = jnp.where(row == at % 8, value, groups[at // 8])
    turned[...] = jnp.concatenate(groups, axis=0).T
    table = jnp.zeros((32, 128), F32)
    for p in range(4):
        table = table + pltpu.roll(turned[pixels(p), :], 2 * p, 1)
    sums[...] = table
    for move in moves[4:]:
        move.wait()
    parts = []
    for i in range(2):
        for j in range(2):
            parts += split_pixels(halves.at[i], j)
    for p in range(8):
        fields[p] = parts[p]
    acc = []
    for q in range(8):
        block = mixing[q]
        total = block[0:1, :] * parts[0]
        for p in range(1, 8):
            total = total + block[p : p + 1, :] * parts[p]
        acc.append(total)
    taps(acc, coarse[...], [kernels[t] for t in range(9)])
    for q in range(8):
        base[q] = acc[q]


def sides(odd, even):
    first = (lax.axis_index("ang") & 1) == 0
    return jnp.where(first, odd, even), jnp.where(first, even, odd)


def forward(coarse, odd, even, base, kernels, stars, sums, dens, prod, table):
    shard = lax.axis_index("rad")
    step = 1.0 / 1024
    acc = [base[q] for q in range(8)]
    place = lax.axis_index("ang")
    met = (place > 0) & (place < lax.axis_size("ang") - 1)
    low, high = sides(jnp.where(met, odd[...], 0.0), even[...])
    here = pl.ds(pl.multiple_of(shard * 128, 128), 128)
    taps(acc, low, [kernels[t, :, here] for t in range(9)])
    taps(acc, high, [kernels[t, :, here] for t in range(18, 27)])
    lane = lanes((32, 128))
    out = sums[...]
    for q in range(8):
        out = jnp.where(lane == q, acc[q][:, 0:1], out)
        out = jnp.where(lane == 8 + q, acc[q][:, 127:128], out)
    for u, value in enumerate((low, coarse[...], high)):
        out = jnp.where(lane == 32 + u, value[:, 0:1], out)
        out = jnp.where(lane == 35 + u, value[:, 127:128], out)
    inner = (lane > 0) & (lane < 127)
    density = []
    for q in range(8):
        d = jnp.exp(acc[q])
        dens[q] = d
        density.append(jnp.where(inner, d, 0.0))
    pairs = jnp.concatenate([density[2 * p] + density[2 * p + 1] for p in range(4)], axis=0)
    strict = (rows((128, 128)) < lanes((128, 128))).astype(F32)
    before = jnp.dot(pairs, strict, precision=HI, preferred_element_type=F32)
    for p in range(4):
        first = before[32 * p : 32 * p + 32] + density[2 * p]
        second = first + density[2 * p + 1]
        first = weighed(step * first, stars[0, pixels(p), :])
        total = second[:, 127:128]
        second = weighed(step * second, stars[1, pixels(p), :])
        prod[2 * p] = first
        prod[2 * p + 1] = second
        share = jnp.sum(first + second, axis=1, keepdims=True)
        for k in range(2):
            out = jnp.where(lane == 16 + 2 * p + k, total, out)
            out = jnp.where(lane == 24 + 2 * p + k, share, out)
    table[...] = out


def weighed(x, w):
    return jnp.where(w != 0.0, x * w, 0.0)


def swap(x):
    even = (rows(x.shape) & 1) == 0
    return jnp.where(even, pltpu.roll(x, x.shape[0] - 1, 0), pltpu.roll(x, 1, 0))


def spread(grad, columns):
    lane = lanes((32, 128))
    plus, minus = [], []
    for q in range(8):
        plus.append(jnp.where(lane == 127, columns[:, 32 + q : 33 + q], grad[q]))
        minus.append(jnp.where(lane == 0, columns[:, 40 + q : 41 + q], grad[q]))
    return minus, grad, plus


def to_row(u, fields, kernels, shard):
    at = pl.ds(pl.multiple_of(shard * 128, 128), 128)
    prev = pl.ds(pl.multiple_of(jnp.maximum(shard - 1, 0) * 128, 128), 128)
    after = pl.ds(pl.multiple_of(jnp.minimum(shard + 1, 3) * 128, 128), 128)
    lane = lanes((8, 128))
    total = None
    for w, field in enumerate(fields):
        part = None
        for v in range(3):
            t = 9 * u + 3 * v + w
            block = kernels[t, :, at]
            if w == 0:
                block = jnp.where(lane == 0, kernels[t, :, after], block)
            if w == 2:
                block = jnp.where(lane == 127, kernels[t, :, prev], block)
            piece = block[0:1, :] * field[0]
            for q in range(1, 8):
                piece = piece + block[q : q + 1, :] * field[q]
            piece = along(piece, 1 - v, 0)
            part = piece if part is None else part + piece
        if w != 1:
            part = pltpu.roll(part, (w - 1) % 128, 1)
        total = part if total is None else total + part
    return total


def middle(prod, stars, kernels, share, weights):
    pairs = jnp.concatenate([prod[2 * p] + prod[2 * p + 1] for p in range(4)], axis=0)
    beyond = (rows((128, 128)) > lanes((128, 128))).astype(F32)
    after = jnp.dot(pairs, beyond, precision=HI, preferred_element_type=F32)
    for p in range(4):
        second = after[32 * p : 32 * p + 32] + prod[2 * p + 1]
        first = second + prod[2 * p]
        for k, value in ((0, first), (1, second)):
            share[2 * p + k] = value - stars[4 + k, pixels(p), :]
    for s in range(4):
        for n in range(9):
            for side in range(2):
                block = kernels[3 * n + 2 * side, :, 128 * s : 128 * s + 128]
                weights[s, side, n] = jnp.broadcast_to(block[:, 127 * side : 127 * side + 1], (8, 128))


def backward(own, by1, by2, by3, dens, share, weights, kernels, stars, grad, edges_out, odd_out, even_out):
    shard = lax.axis_index("rad")
    step = 1.0 / 1024
    even = (rows((8, 128)) & 1) == 0
    held = [own[...], by1[...], by2[...], by3[...]]
    groups = []
    for s in range(4):
        table = held[0]
        for k in range(1, 4):
            table = jnp.where(shard == (s ^ k), held[k], table)
        full = jnp.concatenate([table, jnp.zeros((96, 128), F32)], axis=0).T
        groups.append([full[8 * g : 8 * g + 8] for g in range(9)])
    edges = []
    for s in range(4):
        e = groups[s][4]
        edges.append([along(e, v - 1, 1) for v in range(3)])
    d_low, d_high, totals, shares, whole, tails = [], [], [], [], [], []
    for s in range(4):
        f_low, f_high, t, c, _, w_low, w_high, o_low, _ = groups[s]
        for u in range(3):
            for v in range(3):
                if s > 0:
                    f_low = f_low + weights[s, 0, 3 * u + v] * edges[s - 1][v][3 + u : 4 + u, :]
                if s < 3:
                    f_high = f_high + weights[s, 1, 3 * u + v] * edges[s + 1][v][u : u + 1, :]
        a, b = jnp.exp(f_low), jnp.exp(f_high)
        d_low.append(a)
        d_high.append(b)
        both = a + b
        totals.append(t + both + swap(both))
        tail = step * b * w_high
        tail = tail + swap(tail)
        tails.append(tail)
        head = step * a * w_low
        o_all = jnp.where(even, o_low, swap(o_low))
        shares.append(c - o_all + head + swap(head) + tail)
        whole.append(jnp.where(even, w_low, swap(w_low)))
    zero = jnp.zeros((8, 128), F32)
    nearer = [zero]
    for s in range(3):
        nearer.append(nearer[s] + totals[s])
    nearer = [step * x for x in nearer]
    sums = [shares[s] + weighed(nearer[s], whole[s]) for s in range(4)]
    farther = [zero]
    for s in (3, 2, 1):
        farther.insert(0, farther[0] + sums[s])

    def low_edge(s):
        w, o = groups[s][5], groups[s][7]
        first = weighed(nearer[s] + step * swap(d_low[s]), swap(w) - w) - (swap(o) - o)
        suffix = sums[s] - jnp.where(even, 0.0, first)
        return d_low[s] * step * (farther[s] + suffix)

    def high_edge(s):
        w, o = groups[s][6], groups[s][8]
        last = step * swap(d_high[s]) * (w - swap(w))
        suffix = weighed(nearer[s] + step * totals[s], w) - o - jnp.where(even, last, 0.0)
        return d_high[s] * step * (farther[s] + suffix)

    def mine(values):
        out = values[0]
        for s in range(1, 4):
            out = jnp.where(shard == s, values[s], out)
        return out

    lows = [low_edge(s) for s in range(4)]
    highs = [high_edge(s) for s in range(4)]
    columns = [mine(lows), mine(highs),
               mine([nearer[s] + step * (d_low[s] + swap(d_low[s])) for s in range(4)]),
               mine([farther[s] + tails[s] for s in range(4)]),
               mine([zero] + highs[:3]), mine(lows[1:] + [zero])]
    columns = jnp.concatenate(columns + [jnp.zeros((80, 128), F32)], axis=0).T[0:32]
    edges_out[...] = columns
    lane = lanes((32, 128))
    grads = []
    for p in range(4):
        near, far = columns[:, 16 + 2 * p : 17 + 2 * p], columns[:, 24 + 2 * p : 25 + 2 * p]
        for k in range(2):
            q = 2 * p + k
            suffix = far + weighed(near, stars[2 + k, pixels(p), :]) + share[q]
            g = step * dens[q] * suffix
            g = jnp.where(lane == 0, columns[:, q : q + 1], g)
            g = jnp.where(lane == 127, columns[:, 8 + q : 9 + q], g)
            grad[q] = g
            grads.append(g)
    fields = spread(grads, columns)
    odd, even_row = sides(to_row(0, fields, kernels, shard), to_row(2, fields, kernels, shard))
    odd_out[...] = odd
    even_out[...] = even_row


def finish(grad, columns, fields, kernels, mixing, even, odd, out, own, halves):
    shard = lax.axis_index("rad")
    lane = lanes((32, 128))
    grads = [grad[q] for q in range(8)]
    acc = [fields[p] for p in range(8)]
    for q in range(8):
        block = mixing[q]
        for p in range(8):
            acc[p] = acc[p] + block[p : p + 1, :] * grads[q]
    for i in range(2):
        for j in range(2):
            pair = acc[4 * i + 2 * j : 4 * i + 2 * j + 2]
            half = pl.ds(j, 32, stride=2)
            for side in range(2):
                index = (lane >> 1) + 64 * side
                value = jnp.where((lane & 1) == 0, pick(pair[0], index), pick(pair[1], index))
                halves[side, half, :] = value
        for side in range(2):
            out[i, :, 128 * side : 128 * side + 128] = halves[side]
    place = lax.axis_index("ang")
    other = jnp.where((place & 1) == 0, odd[0:32], odd[32:64])
    met = (place > 0) & (place < lax.axis_size("ang") - 1)
    total = to_row(1, spread(grads, columns[...]), kernels, shard) + even[...]
    own[...] = total + jnp.where(met, other, 0.0)


def call(body, ins, outs, flops, scratch=(), space=pltpu.VMEM):
    shapes = tuple(jax.ShapeDtypeStruct(s, d) for s, d in outs)
    size = sum(x.size * 4 for x in ins) + sum(x.size * 4 for x in shapes)
    return pl.pallas_call(
        body,
        out_shape=shapes,
        in_specs=[pl.BlockSpec(memory_space=space)] * len(ins),
        out_specs=tuple([VMEM] * len(shapes)),
        scratch_shapes=list(scratch),
        cost_estimate=pl.CostEstimate(flops=flops, bytes_accessed=size, transcendentals=0),
        compiler_params=pltpu.CompilerParams(vmem_limit_bytes=16 << 20),
    )(*ins)


def per_device(coarse, excite, kernels, mixing, star_bin, star_count, star_obs, star_isig):
    count = lax.axis_size("ang")
    pairs = [[], []]
    for i in range(count - 1):
        pairs[i % 2] += [(i, i + 1), (i + 1, i)]

    own = coarse[0, 0]
    near = lax.axis_size("rad")
    hops = [(a * near + r, b * near + r) for a, b in pairs[1] for r in range(near)]
    hops += [(a * near + r, a * near + (r ^ 1)) for a in (0, count - 1) for r in range(near)]
    odd = lax.ppermute(own, ("ang", "rad"), hops)
    even = lax.ppermute(own, "ang", pairs[0])
    block = ((8, 32, 128), F32)
    row = ((32, 128), F32)
    stars = [x.transpose(0, 2, 1) for x in (star_bin, star_obs, star_isig)]
    base, fields, stars, sums, mixing_here = call(
        prepare,
        [pltpu.with_memory_space_constraint(x, pltpu.HBM) for x in
         (own, excite[0], kernels, mixing, stars[0], star_count, stars[1], stars[2])],
        (block, block, ((6, 128, 128), F32), row, ((8, 8, 128), F32)), 4_000_000,
        [pltpu.VMEM((128, 128), F32), pltpu.VMEM((2, 2, 64, 128), F32), pltpu.VMEM((32, 128), F32),
         pltpu.VMEM((9, 8, 128), F32), pltpu.VMEM((2, 16, 64), jnp.int32), pltpu.VMEM((2, 64), jnp.int32),
         pltpu.VMEM((2, 16, 64), F32), pltpu.VMEM((2, 16, 64), F32), pltpu.SemaphoreType.DMA((11,))],
        pltpu.HBM,
    )
    dens, prod, table = call(
        forward, (own, odd, even, base, kernels, stars, sums),
        (block, block, row), 6_000_000,
    )
    others = [lax.ppermute(table, "rad", [(i, i ^ k) for i in range(4)]) for k in (1, 2, 3)]
    share, weights = call(
        middle, (prod, stars, kernels), (block, ((4, 2, 9, 8, 128), F32)), 1_000_000,
    )
    grad, columns, odd, even = call(
        backward, (table, *others, dens, share, weights, kernels, stars),
        (block, row, row, row), 8_000_000,
    )
    even = lax.ppermute(even, "ang", pairs[0])
    near = lax.axis_size("rad")
    groups = [[i * near + r, (i + 1) * near + r] for i in range(1, count - 1, 2) for r in range(near)]
    groups += [[i * near + r, i * near + r + 1] for i in (0, count - 1) for r in range(0, near, 2)]
    odd = lax.all_gather(odd, ("ang", "rad"), axis_index_groups=groups, tiled=True)
    grad_excite, grad_coarse = call(
        finish, (grad, columns, fields, kernels, mixing_here, even, odd),
        (((2, 64, 256), F32), row), 4_000_000,
        [pltpu.VMEM((2, 64, 128), F32)],
    )
    return grad_excite[None], grad_coarse[None, None]


def solution(mesh):
    in_specs = (
        P(None, "ang", None, "rad"),
        P(None, "ang", None, "rad"),
        P(),
        P(),
        P("ang", None, None),
        P("ang", None),
        P("ang", None, None),
        P("ang", None, None),
    )
    out_specs = (P(None, "ang", None, "rad"), P(None, "ang", None, "rad"))
    return jax.shard_map(
        per_device, mesh=mesh, in_specs=in_specs, out_specs=out_specs, check_vma=False
    )
```

```python
import jax
import jax.numpy as jnp
from jax import lax
from jax.experimental import pallas as pl
from jax.experimental.pallas import tpu as pltpu
from jax.sharding import PartitionSpec as P


F32 = jnp.float32
HI = lax.Precision.HIGHEST
VMEM = pl.BlockSpec(memory_space=pltpu.VMEM)


def lanes(shape):
    return lax.broadcasted_iota(jnp.int32, shape, 1)


def rows(shape):
    return lax.broadcasted_iota(jnp.int32, shape, 0)


def along(x, k, axis):
    if k == 0:
        return x
    n = x.shape[axis]
    at = lax.broadcasted_iota(jnp.int32, x.shape, axis)
    inside = at < n - k if k > 0 else at >= -k
    return jnp.where(inside, pltpu.roll(x, (-k) % n, axis), 0.0)


def pick(x, index):
    return jnp.take_along_axis(x, index, axis=1, mode="promise_in_bounds")


def split_pixels(ref, j):
    half = pl.ds(j, 32, stride=2)
    low, high = ref[0, half, :], ref[1, half, :]
    lane = lanes((32, 128))
    out = []
    for k in range(2):
        index = (2 * lane + k) & 127
        out.append(jnp.where(lane < 64, pick(low, index), pick(high, index)))
    return out


def pixels(p):
    return pl.ds(64 * (p // 2) + p % 2, 32, stride=2)


def taps(acc, row, weights):
    for w in range(3):
        moved = along(row, w - 1, 1)
        for v in range(3):
            window = along(moved, v - 1, 0)
            block = weights[3 * v + w]
            for q in range(8):
                acc[q] = acc[q] + block[q : q + 1, :] * window


def prepare(coarse_in, excite_in, kernels_in, mixing_in, bin_in, count_in, obs_in, isig_in,
            base, fields, stars, sums, mixing,
            turned, halves, coarse, kernels, star_bin, star_count, star_obs, star_isig, arrived):
    shard = lax.axis_index("rad")
    here = pl.ds(pl.multiple_of(shard * 128, 128), 128)
    moves = [(bin_in, star_bin), (count_in, star_count), (obs_in, star_obs), (isig_in, star_isig)]
    for i in range(2):
        for side in range(2):
            moves.append((excite_in.at[i, :, 128 * side : 128 * side + 128], halves.at[i, side]))
    moves += [(mixing_in.at[:, :, here], mixing), (coarse_in, coarse), (kernels_in.at[9:18, :, here], kernels)]
    moves = [pltpu.make_async_copy(a, b, arrived.at[n]) for n, (a, b) in enumerate(moves)]
    for move in moves:
        move.start()
    for move in moves[:4]:
        move.wait()

    def joined(x):
        return jnp.concatenate([x[0], x[1]], axis=1)

    count = jnp.concatenate([star_count[0:1, :], star_count[1:2, :]], axis=1)
    rel = joined(star_bin) - 256 * shard
    live = (rows((16, 128)) < count) & (rel >= 0) & (rel < 256)
    isig = joined(star_isig)
    w = jnp.where(live, isig * isig, 0.0)
    o = w * joined(star_obs)
    rel = jnp.where(live, rel, -1)
    hits = [[[], []], [[], []]]
    for tile in range(16):
        bin0 = 2 * (rows((8, 128)) + 8 * tile)
        bin1 = bin0 + 1
        total = [[jnp.zeros((8, 128), F32)] * 2 for _ in range(2)]
        for m in range(16):
            at = rel[m : m + 1, :]
            for k, bins in ((0, bin0), (1, bin1)):
                here_now = at == bins
                for f, value in ((0, w), (1, o)):
                    total[f][k] = total[f][k] + jnp.where(here_now, value[m : m + 1, :], 0.0)
        for f in range(2):
            for k in range(2):
                hits[f][k].append(total[f][k])
    hits = [[jnp.concatenate(hits[f][k], axis=0) for k in range(2)] for f in range(2)]
    pairs = jnp.concatenate([hits[f][0] + hits[f][1] for f in range(2)], axis=1)
    beyond = (lanes((128, 128)) > rows((128, 128))).astype(F32)
    after = jnp.dot(beyond, pairs, precision=HI, preferred_element_type=F32)
    ends = []
    for f in range(2):
        second = after[:, 128 * f : 128 * f + 128] + hits[f][1]
        first = second + hits[f][0]
        for k, value in ((0, first), (1, second)):
            stars[2 + 2 * f + k] = value.T
            ends.append((40 + 16 * f + k, value[0:1, :]))
            ends.append((48 + 16 * f + k, value[127:128, :]))
    for k in range(2):
        stars[k] = hits[0][k].T
    row = rows((8, 128))
    groups = [jnp.zeros((8, 128), F32)] * 16
    for at, value in ends:
        groups[at // 8] = jnp.where(row == at % 8, value, groups[at // 8])
    turned[...] = jnp.concatenate(groups, axis=0).T
    table = jnp.zeros((32, 128), F32)
    for p in range(4):
        table = table + pltpu.roll(turned[pixels(p), :], 2 * p, 1)
    sums[...] = table
    for move in moves[4:]:
        move.wait()
    parts = []
    for i in range(2):
        for j in range(2):
            parts += split_pixels(halves.at[i], j)
    for p in range(8):
        fields[p] = parts[p]
    acc = []
    for q in range(8):
        block = mixing[q]
        total = block[0:1, :] * parts[0]
        for p in range(1, 8):
            total = total + block[p : p + 1, :] * parts[p]
        acc.append(total)
    taps(acc, coarse[...], [kernels[t] for t in range(9)])
    for q in range(8):
        base[q] = acc[q]


def sides(odd, even):
    first = (lax.axis_index("ang") & 1) == 0
    return jnp.where(first, odd, even), jnp.where(first, even, odd)


def forward(coarse, odd, even, base, kernels, stars, sums, dens, prod, table):
    shard = lax.axis_index("rad")
    step = 1.0 / 1024
    acc = [base[q] for q in range(8)]
    place = lax.axis_index("ang")
    met = (place > 0) & (place < lax.axis_size("ang") - 1)
    low, high = sides(jnp.where(met, odd[...], 0.0), even[...])
    here = pl.ds(pl.multiple_of(shard * 128, 128), 128)
    taps(acc, low, [kernels[t, :, here] for t in range(9)])
    taps(acc, high, [kernels[t, :, here] for t in range(18, 27)])
    lane = lanes((32, 128))
    out = sums[...]
    for q in range(8):
        out = jnp.where(lane == q, acc[q][:, 0:1], out)
        out = jnp.where(lane == 8 + q, acc[q][:, 127:128], out)
    for u, value in enumerate((low, coarse[...], high)):
        out = jnp.where(lane == 32 + u, value[:, 0:1], out)
        out = jnp.where(lane == 35 + u, value[:, 127:128], out)
    inner = (lane > 0) & (lane < 127)
    density = []
    for q in range(8):
        d = jnp.exp(acc[q])
        dens[q] = d
        density.append(jnp.where(inner, d, 0.0))
    pairs = jnp.concatenate([density[2 * p] + density[2 * p + 1] for p in range(4)], axis=0)
    strict = (rows((128, 128)) < lanes((128, 128))).astype(F32)
    before = jnp.dot(pairs, strict, precision=HI, preferred_element_type=F32)
    for p in range(4):
        first = before[32 * p : 32 * p + 32] + density[2 * p]
        second = first + density[2 * p + 1]
        first = weighed(step * first, stars[0, pixels(p), :])
        total = second[:, 127:128]
        second = weighed(step * second, stars[1, pixels(p), :])
        prod[2 * p] = first
        prod[2 * p + 1] = second
        share = jnp.sum(first + second, axis=1, keepdims=True)
        for k in range(2):
            out = jnp.where(lane == 16 + 2 * p + k, total, out)
            out = jnp.where(lane == 24 + 2 * p + k, share, out)
    table[...] = out


def weighed(x, w):
    return jnp.where(w != 0.0, x * w, 0.0)


def swap(x):
    even = (rows(x.shape) & 1) == 0
    return jnp.where(even, pltpu.roll(x, x.shape[0] - 1, 0), pltpu.roll(x, 1, 0))


def spread(grad, columns):
    lane = lanes((32, 128))
    plus, minus = [], []
    for q in range(8):
        plus.append(jnp.where(lane == 127, columns[:, 32 + q : 33 + q], grad[q]))
        minus.append(jnp.where(lane == 0, columns[:, 40 + q : 41 + q], grad[q]))
    return minus, grad, plus


def to_row(u, fields, kernels, shard):
    at = pl.ds(pl.multiple_of(shard * 128, 128), 128)
    prev = pl.ds(pl.multiple_of(jnp.maximum(shard - 1, 0) * 128, 128), 128)
    after = pl.ds(pl.multiple_of(jnp.minimum(shard + 1, 3) * 128, 128), 128)
    lane = lanes((8, 128))
    total = None
    for w, field in enumerate(fields):
        part = None
        for v in range(3):
            t = 9 * u + 3 * v + w
            block = kernels[t, :, at]
            if w == 0:
                block = jnp.where(lane == 0, kernels[t, :, after], block)
            if w == 2:
                block = jnp.where(lane == 127, kernels[t, :, prev], block)
            piece = block[0:1, :] * field[0]
            for q in range(1, 8):
                piece = piece + block[q : q + 1, :] * field[q]
            piece = along(piece, 1 - v, 0)
            part = piece if part is None else part + piece
        if w != 1:
            part = pltpu.roll(part, (w - 1) % 128, 1)
        total = part if total is None else total + part
    return total


def middle(prod, stars, kernels, share, weights):
    pairs = jnp.concatenate([prod[2 * p] + prod[2 * p + 1] for p in range(4)], axis=0)
    beyond = (rows((128, 128)) > lanes((128, 128))).astype(F32)
    after = jnp.dot(pairs, beyond, precision=HI, preferred_element_type=F32)
    for p in range(4):
        second = after[32 * p : 32 * p + 32] + prod[2 * p + 1]
        first = second + prod[2 * p]
        for k, value in ((0, first), (1, second)):
            share[2 * p + k] = value - stars[4 + k, pixels(p), :]
    for s in range(4):
        for n in range(9):
            for side in range(2):
                block = kernels[3 * n + 2 * side, :, 128 * s : 128 * s + 128]
                weights[s, side, n] = jnp.broadcast_to(block[:, 127 * side : 127 * side + 1], (8, 128))


def backward(own, by1, by2, by3, dens, share, weights, kernels, stars, grad, edges_out, odd_out, even_out):
    shard = lax.axis_index("rad")
    step = 1.0 / 1024
    even = (rows((8, 128)) & 1) == 0
    held = [own[...], by1[...], by2[...], by3[...]]
    groups = []
    for s in range(4):
        table = held[0]
        for k in range(1, 4):
            table = jnp.where(shard == (s ^ k), held[k], table)
        full = jnp.concatenate([table, jnp.zeros((96, 128), F32)], axis=0).T
        groups.append([full[8 * g : 8 * g + 8] for g in range(9)])
    edges = []
    for s in range(4):
        e = groups[s][4]
        edges.append([along(e, v - 1, 1) for v in range(3)])
    d_low, d_high, totals, shares, whole, tails = [], [], [], [], [], []
    for s in range(4):
        f_low, f_high, t, c, _, w_low, w_high, o_low, _ = groups[s]
        for u in range(3):
            for v in range(3):
                if s > 0:
                    f_low = f_low + weights[s, 0, 3 * u + v] * edges[s - 1][v][3 + u : 4 + u, :]
                if s < 3:
                    f_high = f_high + weights[s, 1, 3 * u + v] * edges[s + 1][v][u : u + 1, :]
        a, b = jnp.exp(f_low), jnp.exp(f_high)
        d_low.append(a)
        d_high.append(b)
        both = a + b
        totals.append(t + both + swap(both))
        tail = step * b * w_high
        tail = tail + swap(tail)
        tails.append(tail)
        head = step * a * w_low
        o_all = jnp.where(even, o_low, swap(o_low))
        shares.append(c - o_all + head + swap(head) + tail)
        whole.append(jnp.where(even, w_low, swap(w_low)))
    zero = jnp.zeros((8, 128), F32)
    nearer = [zero]
    for s in range(3):
        nearer.append(nearer[s] + totals[s])
    nearer = [step * x for x in nearer]
    sums = [shares[s] + weighed(nearer[s], whole[s]) for s in range(4)]
    farther = [zero]
    for s in (3, 2, 1):
        farther.insert(0, farther[0] + sums[s])

    def low_edge(s):
        w, o = groups[s][5], groups[s][7]
        first = weighed(nearer[s] + step * swap(d_low[s]), swap(w) - w) - (swap(o) - o)
        suffix = sums[s] - jnp.where(even, 0.0, first)
        return d_low[s] * step * (farther[s] + suffix)

    def high_edge(s):
        w, o = groups[s][6], groups[s][8]
        last = step * swap(d_high[s]) * (w - swap(w))
        suffix = weighed(nearer[s] + step * totals[s], w) - o - jnp.where(even, last, 0.0)
        return d_high[s] * step * (farther[s] + suffix)

    def mine(values):
        out = values[0]
        for s in range(1, 4):
            out = jnp.where(shard == s, values[s], out)
        return out

    lows = [low_edge(s) for s in range(4)]
    highs = [high_edge(s) for s in range(4)]
    columns = [mine(lows), mine(highs),
               mine([nearer[s] + step * (d_low[s] + swap(d_low[s])) for s in range(4)]),
               mine([farther[s] + tails[s] for s in range(4)]),
               mine([zero] + highs[:3]), mine(lows[1:] + [zero])]
    columns = jnp.concatenate(columns + [jnp.zeros((80, 128), F32)], axis=0).T[0:32]
    edges_out[...] = columns
    lane = lanes((32, 128))
    grads = []
    for p in range(4):
        near, far = columns[:, 16 + 2 * p : 17 + 2 * p], columns[:, 24 + 2 * p : 25 + 2 * p]
        for k in range(2):
            q = 2 * p + k
            suffix = far + weighed(near, stars[2 + k, pixels(p), :]) + share[q]
            g = step * dens[q] * suffix
            g = jnp.where(lane == 0, columns[:, q : q + 1], g)
            g = jnp.where(lane == 127, columns[:, 8 + q : 9 + q], g)
            grad[q] = g
            grads.append(g)
    fields = spread(grads, columns)
    odd, even_row = sides(to_row(0, fields, kernels, shard), to_row(2, fields, kernels, shard))
    odd_out[...] = odd
    even_out[...] = even_row


def finish(grad, columns, fields, kernels, mixing, out, own, halves):
    shard = lax.axis_index("rad")
    lane = lanes((32, 128))
    grads = [grad[q] for q in range(8)]
    acc = [fields[p] for p in range(8)]
    for q in range(8):
        block = mixing[q]
        for p in range(8):
            acc[p] = acc[p] + block[p : p + 1, :] * grads[q]
    for i in range(2):
        for j in range(2):
            pair = acc[4 * i + 2 * j : 4 * i + 2 * j + 2]
            half = pl.ds(j, 32, stride=2)
            for side in range(2):
                index = (lane >> 1) + 64 * side
                value = jnp.where((lane & 1) == 0, pick(pair[0], index), pick(pair[1], index))
                halves[side, half, :] = value
        for side in range(2):
            out[i, :, 128 * side : 128 * side + 128] = halves[side]
    own[...] = to_row(1, spread(grads, columns[...]), kernels, shard)


def total(own, even, odd, out):
    place = lax.axis_index("ang")
    met = (place > 0) & (place < lax.axis_size("ang") - 1)
    out[...] = own[...] + even[...] + jnp.where(met, odd[...], 0.0)


def call(body, ins, outs, flops, scratch=(), space=pltpu.VMEM):
    shapes = tuple(jax.ShapeDtypeStruct(s, d) for s, d in outs)
    size = sum(x.size * 4 for x in ins) + sum(x.size * 4 for x in shapes)
    return pl.pallas_call(
        body,
        out_shape=shapes,
        in_specs=[pl.BlockSpec(memory_space=space)] * len(ins),
        out_specs=tuple([VMEM] * len(shapes)),
        scratch_shapes=list(scratch),
        cost_estimate=pl.CostEstimate(flops=flops, bytes_accessed=size, transcendentals=0),
        compiler_params=pltpu.CompilerParams(vmem_limit_bytes=16 << 20),
    )(*ins)


def per_device(coarse, excite, kernels, mixing, star_bin, star_count, star_obs, star_isig):
    count = lax.axis_size("ang")
    pairs = [[], []]
    for i in range(count - 1):
        pairs[i % 2] += [(i, i + 1), (i + 1, i)]

    near = lax.axis_size("rad")
    hops = [(a * near + r, b * near + r) for a, b in pairs[1] for r in range(near)]
    hops += [(a * near + r, a * near + (r ^ 1)) for a in (0, count - 1) for r in range(near)]
    own = coarse[0, 0]
    odd = lax.ppermute(own, ("ang", "rad"), hops)
    even = lax.ppermute(own, "ang", pairs[0])
    block = ((8, 32, 128), F32)
    row = ((32, 128), F32)
    stars = [x.transpose(0, 2, 1) for x in (star_bin, star_obs, star_isig)]
    base, fields, stars, sums, mixing_here = call(
        prepare,
        [pltpu.with_memory_space_constraint(x, pltpu.HBM) for x in
         (own, excite[0], kernels, mixing, stars[0], star_count, stars[1], stars[2])],
        (block, block, ((6, 128, 128), F32), row, ((8, 8, 128), F32)), 4_000_000,
        [pltpu.VMEM((128, 128), F32), pltpu.VMEM((2, 2, 64, 128), F32), pltpu.VMEM((32, 128), F32),
         pltpu.VMEM((9, 8, 128), F32), pltpu.VMEM((2, 16, 64), jnp.int32), pltpu.VMEM((2, 64), jnp.int32),
         pltpu.VMEM((2, 16, 64), F32), pltpu.VMEM((2, 16, 64), F32), pltpu.SemaphoreType.DMA((11,))],
        pltpu.HBM,
    )
    dens, prod, table = call(
        forward, (own, odd, even, base, kernels, stars, sums),
        (block, block, row), 6_000_000,
    )
    others = [lax.ppermute(table, "rad", [(i, i ^ k) for i in range(4)]) for k in (1, 2, 3)]
    share, weights = call(
        middle, (prod, stars, kernels), (block, ((4, 2, 9, 8, 128), F32)), 1_000_000,
    )
    grad, columns, odd, even = call(
        backward, (table, *others, dens, share, weights, kernels, stars),
        (block, row, row, row), 8_000_000,
    )
    even = lax.ppermute(even, "ang", pairs[0])
    odd = lax.ppermute(odd, ("ang", "rad"), hops)
    grad_excite, here = call(
        finish, (grad, columns, fields, kernels, mixing_here),
        (((2, 64, 256), F32), row), 4_000_000,
        [pltpu.VMEM((2, 64, 128), F32)],
    )
    (grad_coarse,) = call(total, (here, even, odd), (row,), 10_000)
    return grad_excite[None], grad_coarse[None, None]


def solution(mesh):
    in_specs = (
        P(None, "ang", None, "rad"),
        P(None, "ang", None, "rad"),
        P(),
        P(),
        P("ang", None, None),
        P("ang", None),
        P("ang", None, None),
        P("ang", None, None),
    )
    out_specs = (P(None, "ang", None, "rad"), P(None, "ang", None, "rad"))
    return jax.shard_map(
        per_device, mesh=mesh, in_specs=in_specs, out_specs=out_specs, check_vma=False
    )
```

```python
import jax
import jax.numpy as jnp
from jax import lax
from jax.experimental import pallas as pl
from jax.experimental.pallas import tpu as pltpu
from jax.sharding import PartitionSpec as P


F32 = jnp.float32
HI = lax.Precision.HIGHEST
VMEM = pl.BlockSpec(memory_space=pltpu.VMEM)


def lanes(shape):
    return lax.broadcasted_iota(jnp.int32, shape, 1)


def rows(shape):
    return lax.broadcasted_iota(jnp.int32, shape, 0)


def along(x, k, axis):
    if k == 0:
        return x
    n = x.shape[axis]
    at = lax.broadcasted_iota(jnp.int32, x.shape, axis)
    inside = at < n - k if k > 0 else at >= -k
    return jnp.where(inside, pltpu.roll(x, (-k) % n, axis), 0.0)


def pick(x, index):
    return jnp.take_along_axis(x, index, axis=1, mode="promise_in_bounds")


def split_pixels(ref, j):
    half = pl.ds(j, 32, stride=2)
    low, high = ref[0, half, :], ref[1, half, :]
    lane = lanes((32, 128))
    out = []
    for k in range(2):
        index = (2 * lane + k) & 127
        out.append(jnp.where(lane < 64, pick(low, index), pick(high, index)))
    return out


def pixels(p):
    return pl.ds(64 * (p // 2) + p % 2, 32, stride=2)


def taps(acc, row, weights):
    for w in range(3):
        moved = along(row, w - 1, 1)
        for v in range(3):
            window = along(moved, v - 1, 0)
            block = weights[3 * v + w]
            for q in range(8):
                acc[q] = acc[q] + block[q : q + 1, :] * window


def prepare(coarse_in, excite_in, kernels_in, mixing_in, bin_in, count_in, obs_in, isig_in,
            base, fields, stars, sums, mixing,
            turned, halves, coarse, kernels, star_bin, star_count, star_obs, star_isig, arrived):
    shard = lax.axis_index("rad")
    here = pl.ds(pl.multiple_of(shard * 128, 128), 128)
    moves = [(bin_in, star_bin), (count_in, star_count), (obs_in, star_obs), (isig_in, star_isig)]
    for i in range(2):
        for side in range(2):
            moves.append((excite_in.at[i, :, 128 * side : 128 * side + 128], halves.at[i, side]))
    moves += [(mixing_in.at[:, :, here], mixing), (coarse_in, coarse), (kernels_in.at[9:18, :, here], kernels)]
    moves = [pltpu.make_async_copy(a, b, arrived.at[n]) for n, (a, b) in enumerate(moves)]
    for move in moves:
        move.start()
    for move in moves[:4]:
        move.wait()

    def joined(x):
        return jnp.concatenate([x[0], x[1]], axis=1)

    count = jnp.concatenate([star_count[0:1, :], star_count[1:2, :]], axis=1)
    rel = joined(star_bin) - 256 * shard
    live = (rows((16, 128)) < count) & (rel >= 0) & (rel < 256)
    isig = joined(star_isig)
    w = jnp.where(live, isig * isig, 0.0)
    o = w * joined(star_obs)
    rel = jnp.where(live, rel, -1)
    hits = [[[], []], [[], []]]
    for tile in range(16):
        bin0 = 2 * (rows((8, 128)) + 8 * tile)
        bin1 = bin0 + 1
        total = [[jnp.zeros((8, 128), F32)] * 2 for _ in range(2)]
        for m in range(16):
            at = rel[m : m + 1, :]
            for k, bins in ((0, bin0), (1, bin1)):
                here_now = at == bins
                for f, value in ((0, w), (1, o)):
                    total[f][k] = total[f][k] + jnp.where(here_now, value[m : m + 1, :], 0.0)
        for f in range(2):
            for k in range(2):
                hits[f][k].append(total[f][k])
    hits = [[jnp.concatenate(hits[f][k], axis=0) for k in range(2)] for f in range(2)]
    pairs = jnp.concatenate([hits[f][0] + hits[f][1] for f in range(2)], axis=1)
    beyond = (lanes((128, 128)) > rows((128, 128))).astype(F32)
    after = jnp.dot(beyond, pairs, precision=HI, preferred_element_type=F32)
    ends = []
    for f in range(2):
        second = after[:, 128 * f : 128 * f + 128] + hits[f][1]
        first = second + hits[f][0]
        for k, value in ((0, first), (1, second)):
            stars[2 + 2 * f + k] = value.T
            ends.append((40 + 16 * f + k, value[0:1, :]))
            ends.append((48 + 16 * f + k, value[127:128, :]))
    for k in range(2):
        stars[k] = hits[0][k].T
    row = rows((8, 128))
    groups = [jnp.zeros((8, 128), F32)] * 16
    for at, value in ends:
        groups[at // 8] = jnp.where(row == at % 8, value, groups[at // 8])
    turned[...] = jnp.concatenate(groups, axis=0).T
    table = jnp.zeros((32, 128), F32)
    for p in range(4):
        table = table + pltpu.roll(turned[pixels(p), :], 2 * p, 1)
    sums[...] = table
    for move in moves[4:]:
        move.wait()
    parts = []
    for i in range(2):
        for j in range(2):
            parts += split_pixels(halves.at[i], j)
    for p in range(8):
        fields[p] = parts[p]
    acc = []
    for q in range(8):
        block = mixing[q]
        total = block[0:1, :] * parts[0]
        for p in range(1, 8):
            total = total + block[p : p + 1, :] * parts[p]
        acc.append(total)
    taps(acc, coarse[...], [kernels[t] for t in range(9)])
    for q in range(8):
        base[q] = acc[q]


def sides(odd, even):
    first = (lax.axis_index("ang") & 1) == 0
    return jnp.where(first, odd, even), jnp.where(first, even, odd)


def forward(coarse, odd, even, base, kernels, stars, sums, dens, table):
    shard = lax.axis_index("rad")
    step = 1.0 / 1024
    acc = [base[q] for q in range(8)]
    place = lax.axis_index("ang")
    met = (place > 0) & (place < lax.axis_size("ang") - 1)
    low, high = sides(jnp.where(met, odd[...], 0.0), even[...])
    here = pl.ds(pl.multiple_of(shard * 128, 128), 128)
    taps(acc, low, [kernels[t, :, here] for t in range(9)])
    taps(acc, high, [kernels[t, :, here] for t in range(18, 27)])
    lane = lanes((32, 128))
    out = sums[...]
    for q in range(8):
        out = jnp.where(lane == q, acc[q][:, 0:1], out)
        out = jnp.where(lane == 8 + q, acc[q][:, 127:128], out)
    for u, value in enumerate((low, coarse[...], high)):
        out = jnp.where(lane == 32 + u, value[:, 0:1], out)
        out = jnp.where(lane == 35 + u, value[:, 127:128], out)
    inner = (lane > 0) & (lane < 127)
    density = []
    for q in range(8):
        d = jnp.exp(acc[q])
        dens[q] = d
        density.append(jnp.where(inner, d, 0.0))
    for p in range(4):
        first, second = density[2 * p], density[2 * p + 1]
        share = weighed(first, stars[2, pixels(p), :]) + weighed(second, stars[3, pixels(p), :])
        total = jnp.sum(first + second, axis=1, keepdims=True)
        share = step * jnp.sum(share, axis=1, keepdims=True)
        for k in range(2):
            out = jnp.where(lane == 16 + 2 * p + k, total, out)
            out = jnp.where(lane == 24 + 2 * p + k, share, out)
    table[...] = out


def weighed(x, w):
    return jnp.where(w != 0.0, x * w, 0.0)


def swap(x):
    even = (rows(x.shape) & 1) == 0
    return jnp.where(even, pltpu.roll(x, x.shape[0] - 1, 0), pltpu.roll(x, 1, 0))


def spread(grad, columns):
    lane = lanes((32, 128))
    plus, minus = [], []
    for q in range(8):
        plus.append(jnp.where(lane == 127, columns[:, 32 + q : 33 + q], grad[q]))
        minus.append(jnp.where(lane == 0, columns[:, 40 + q : 41 + q], grad[q]))
    return minus, grad, plus


def to_row(u, fields, kernels, shard):
    at = pl.ds(pl.multiple_of(shard * 128, 128), 128)
    prev = pl.ds(pl.multiple_of(jnp.maximum(shard - 1, 0) * 128, 128), 128)
    after = pl.ds(pl.multiple_of(jnp.minimum(shard + 1, 3) * 128, 128), 128)
    lane = lanes((8, 128))
    total = None
    for w, field in enumerate(fields):
        part = None
        for v in range(3):
            t = 9 * u + 3 * v + w
            block = kernels[t, :, at]
            if w == 0:
                block = jnp.where(lane == 0, kernels[t, :, after], block)
            if w == 2:
                block = jnp.where(lane == 127, kernels[t, :, prev], block)
            piece = block[0:1, :] * field[0]
            for q in range(1, 8):
                piece = piece + block[q : q + 1, :] * field[q]
            piece = along(piece, 1 - v, 0)
            part = piece if part is None else part + piece
        if w != 1:
            part = pltpu.roll(part, (w - 1) % 128, 1)
        total = part if total is None else total + part
    return total


def middle(dens, stars, kernels, share, weights):
    step = 1.0 / 1024
    lane = lanes((32, 128))
    inner = (lane > 0) & (lane < 127)
    density = [jnp.where(inner, dens[q], 0.0) for q in range(8)]
    pairs = jnp.concatenate([density[2 * p] + density[2 * p + 1] for p in range(4)], axis=0)
    strict = (rows((128, 128)) < lanes((128, 128))).astype(F32)
    before = jnp.dot(pairs, strict, precision=HI, preferred_element_type=F32)
    prod = []
    for p in range(4):
        first = before[32 * p : 32 * p + 32] + density[2 * p]
        second = first + density[2 * p + 1]
        prod.append(weighed(step * first, stars[0, pixels(p), :]))
        prod.append(weighed(step * second, stars[1, pixels(p), :]))
    pairs = jnp.concatenate([prod[2 * p] + prod[2 * p + 1] for p in range(4)], axis=0)
    beyond = (rows((128, 128)) > lanes((128, 128))).astype(F32)
    after = jnp.dot(pairs, beyond, precision=HI, preferred_element_type=F32)
    for p in range(4):
        second = after[32 * p : 32 * p + 32] + prod[2 * p + 1]
        first = second + prod[2 * p]
        for k, value in ((0, first), (1, second)):
            share[2 * p + k] = value - stars[4 + k, pixels(p), :]
    for s in range(4):
        for n in range(9):
            for side in range(2):
                block = kernels[3 * n + 2 * side, :, 128 * s : 128 * s + 128]
                weights[s, side, n] = jnp.broadcast_to(block[:, 127 * side : 127 * side + 1], (8, 128))


def backward(own, by1, by2, by3, dens, share, weights, kernels, stars, grad, edges_out, odd_out, even_out):
    shard = lax.axis_index("rad")
    step = 1.0 / 1024
    even = (rows((8, 128)) & 1) == 0
    held = [own[...], by1[...], by2[...], by3[...]]
    groups = []
    for s in range(4):
        table = held[0]
        for k in range(1, 4):
            table = jnp.where(shard == (s ^ k), held[k], table)
        full = jnp.concatenate([table, jnp.zeros((96, 128), F32)], axis=0).T
        groups.append([full[8 * g : 8 * g + 8] for g in range(9)])
    edges = []
    for s in range(4):
        e = groups[s][4]
        edges.append([along(e, v - 1, 1) for v in range(3)])
    d_low, d_high, totals, shares, whole, tails = [], [], [], [], [], []
    for s in range(4):
        f_low, f_high, t, c, _, w_low, w_high, o_low, _ = groups[s]
        for u in range(3):
            for v in range(3):
                if s > 0:
                    f_low = f_low + weights[s, 0, 3 * u + v] * edges[s - 1][v][3 + u : 4 + u, :]
                if s < 3:
                    f_high = f_high + weights[s, 1, 3 * u + v] * edges[s + 1][v][u : u + 1, :]
        a, b = jnp.exp(f_low), jnp.exp(f_high)
        d_low.append(a)
        d_high.append(b)
        both = a + b
        totals.append(t + both + swap(both))
        tail = step * b * w_high
        tail = tail + swap(tail)
        tails.append(tail)
        head = step * a * w_low
        o_all = jnp.where(even, o_low, swap(o_low))
        shares.append(c - o_all + head + swap(head) + tail)
        whole.append(jnp.where(even, w_low, swap(w_low)))
    zero = jnp.zeros((8, 128), F32)
    nearer = [zero]
    for s in range(3):
        nearer.append(nearer[s] + totals[s])
    nearer = [step * x for x in nearer]
    sums = [shares[s] + weighed(nearer[s], whole[s]) for s in range(4)]
    farther = [zero]
    for s in (3, 2, 1):
        farther.insert(0, farther[0] + sums[s])

    def low_edge(s):
        w, o = groups[s][5], groups[s][7]
        first = weighed(nearer[s] + step * swap(d_low[s]), swap(w) - w) - (swap(o) - o)
        suffix = sums[s] - jnp.where(even, 0.0, first)
        return d_low[s] * step * (farther[s] + suffix)

    def high_edge(s):
        w, o = groups[s][6], groups[s][8]
        last = step * swap(d_high[s]) * (w - swap(w))
        suffix = weighed(nearer[s] + step * totals[s], w) - o - jnp.where(even, last, 0.0)
        return d_high[s] * step * (farther[s] + suffix)

    def mine(values):
        out = values[0]
        for s in range(1, 4):
            out = jnp.where(shard == s, values[s], out)
        return out

    lows = [low_edge(s) for s in range(4)]
    highs = [high_edge(s) for s in range(4)]
    columns = [mine(lows), mine(highs),
               mine([nearer[s] + step * (d_low[s] + swap(d_low[s])) for s in range(4)]),
               mine([farther[s] + tails[s] for s in range(4)]),
               mine([zero] + highs[:3]), mine(lows[1:] + [zero])]
    columns = jnp.concatenate(columns + [jnp.zeros((80, 128), F32)], axis=0).T[0:32]
    edges_out[...] = columns
    lane = lanes((32, 128))
    grads = []
    for p in range(4):
        near, far = columns[:, 16 + 2 * p : 17 + 2 * p], columns[:, 24 + 2 * p : 25 + 2 * p]
        for k in range(2):
            q = 2 * p + k
            suffix = far + weighed(near, stars[2 + k, pixels(p), :]) + share[q]
            g = step * dens[q] * suffix
            g = jnp.where(lane == 0, columns[:, q : q + 1], g)
            g = jnp.where(lane == 127, columns[:, 8 + q : 9 + q], g)
            grad[q] = g
            grads.append(g)
    fields = spread(grads, columns)
    odd, even_row = sides(to_row(0, fields, kernels, shard), to_row(2, fields, kernels, shard))
    odd_out[...] = odd
    even_out[...] = even_row


def finish(grad, columns, fields, kernels, mixing, out, own, halves):
    shard = lax.axis_index("rad")
    lane = lanes((32, 128))
    grads = [grad[q] for q in range(8)]
    acc = [fields[p] for p in range(8)]
    for q in range(8):
        block = mixing[q]
        for p in range(8):
            acc[p] = acc[p] + block[p : p + 1, :] * grads[q]
    for i in range(2):
        for j in range(2):
            pair = acc[4 * i + 2 * j : 4 * i + 2 * j + 2]
            half = pl.ds(j, 32, stride=2)
            for side in range(2):
                index = (lane >> 1) + 64 * side
                value = jnp.where((lane & 1) == 0, pick(pair[0], index), pick(pair[1], index))
                halves[side, half, :] = value
        for side in range(2):
            out[i, :, 128 * side : 128 * side + 128] = halves[side]
    own[...] = to_row(1, spread(grads, columns[...]), kernels, shard)


def total(own, even, odd, out):
    place = lax.axis_index("ang")
    met = (place > 0) & (place < lax.axis_size("ang") - 1)
    out[...] = own[...] + even[...] + jnp.where(met, odd[...], 0.0)


def call(body, ins, outs, flops, scratch=(), space=pltpu.VMEM):
    shapes = tuple(jax.ShapeDtypeStruct(s, d) for s, d in outs)
    size = sum(x.size * 4 for x in ins) + sum(x.size * 4 for x in shapes)
    return pl.pallas_call(
        body,
        out_shape=shapes,
        in_specs=[pl.BlockSpec(memory_space=space)] * len(ins),
        out_specs=tuple([VMEM] * len(shapes)),
        scratch_shapes=list(scratch),
        cost_estimate=pl.CostEstimate(flops=flops, bytes_accessed=size, transcendentals=0),
        compiler_params=pltpu.CompilerParams(vmem_limit_bytes=16 << 20),
    )(*ins)


def per_device(coarse, excite, kernels, mixing, star_bin, star_count, star_obs, star_isig):
    count = lax.axis_size("ang")
    pairs = [[], []]
    for i in range(count - 1):
        pairs[i % 2] += [(i, i + 1), (i + 1, i)]

    near = lax.axis_size("rad")
    hops = [(a * near + r, b * near + r) for a, b in pairs[1] for r in range(near)]
    hops += [(a * near + r, a * near + (r ^ 1)) for a in (0, count - 1) for r in range(near)]
    own = coarse[0, 0]
    odd = lax.ppermute(own, ("ang", "rad"), hops)
    even = lax.ppermute(own, "ang", pairs[0])
    block = ((8, 32, 128), F32)
    row = ((32, 128), F32)
    stars = [x.transpose(0, 2, 1) for x in (star_bin, star_obs, star_isig)]
    base, fields, stars, sums, mixing_here = call(
        prepare,
        [pltpu.with_memory_space_constraint(x, pltpu.HBM) for x in
         (own, excite[0], kernels, mixing, stars[0], star_count, stars[1], stars[2])],
        (block, block, ((6, 128, 128), F32), row, ((8, 8, 128), F32)), 4_000_000,
        [pltpu.VMEM((128, 128), F32), pltpu.VMEM((2, 2, 64, 128), F32), pltpu.VMEM((32, 128), F32),
         pltpu.VMEM((9, 8, 128), F32), pltpu.VMEM((2, 16, 64), jnp.int32), pltpu.VMEM((2, 64), jnp.int32),
         pltpu.VMEM((2, 16, 64), F32), pltpu.VMEM((2, 16, 64), F32), pltpu.SemaphoreType.DMA((11,))],
        pltpu.HBM,
    )
    dens, table = call(
        forward, (own, odd, even, base, kernels, stars, sums),
        (block, row), 6_000_000,
    )
    others = [lax.ppermute(table, "rad", [(i, i ^ k) for i in range(4)]) for k in (1, 2, 3)]
    share, weights = call(
        middle, (dens, stars, kernels), (block, ((4, 2, 9, 8, 128), F32)), 1_000_000,
    )
    grad, columns, odd, even = call(
        backward, (table, *others, dens, share, weights, kernels, stars),
        (block, row, row, row), 8_000_000,
    )
    even = lax.ppermute(even, "ang", pairs[0])
    odd = lax.ppermute(odd, ("ang", "rad"), hops)
    grad_excite, here = call(
        finish, (grad, columns, fields, kernels, mixing_here),
        (((2, 64, 256), F32), row), 4_000_000,
        [pltpu.VMEM((2, 64, 128), F32)],
    )
    (grad_coarse,) = call(total, (here, even, odd), (row,), 10_000)
    return grad_excite[None], grad_coarse[None, None]


def solution(mesh):
    in_specs = (
        P(None, "ang", None, "rad"),
        P(None, "ang", None, "rad"),
        P(),
        P(),
        P("ang", None, None),
        P("ang", None),
        P("ang", None, None),
        P("ang", None, None),
    )
    out_specs = (P(None, "ang", None, "rad"), P(None, "ang", None, "rad"))
    return jax.shard_map(
        per_device, mesh=mesh, in_specs=in_specs, out_specs=out_specs, check_vma=False
    )
```

```python
import jax
import jax.numpy as jnp
from jax import lax
from jax.experimental import pallas as pl
from jax.experimental.pallas import tpu as pltpu
from jax.sharding import PartitionSpec as P


F32 = jnp.float32
HI = lax.Precision.HIGHEST
VMEM = pl.BlockSpec(memory_space=pltpu.VMEM)


def lanes(shape):
    return lax.broadcasted_iota(jnp.int32, shape, 1)


def rows(shape):
    return lax.broadcasted_iota(jnp.int32, shape, 0)


def along(x, k, axis):
    if k == 0:
        return x
    n = x.shape[axis]
    at = lax.broadcasted_iota(jnp.int32, x.shape, axis)
    inside = at < n - k if k > 0 else at >= -k
    return jnp.where(inside, pltpu.roll(x, (-k) % n, axis), 0.0)


def pick(x, index):
    return jnp.take_along_axis(x, index, axis=1, mode="promise_in_bounds")


def split_pixels(ref, j):
    half = pl.ds(j, 32, stride=2)
    low, high = ref[0, half, :], ref[1, half, :]
    lane = lanes((32, 128))
    out = []
    for k in range(2):
        index = (2 * lane + k) & 127
        out.append(jnp.where(lane < 64, pick(low, index), pick(high, index)))
    return out


def pixels(p):
    return pl.ds(64 * (p // 2) + p % 2, 32, stride=2)


def taps(acc, row, weights):
    for w in range(3):
        moved = along(row, w - 1, 1)
        for v in range(3):
            window = along(moved, v - 1, 0)
            block = weights[3 * v + w]
            for q in range(8):
                acc[q] = acc[q] + block[q : q + 1, :] * window


def prepare(coarse_in, excite_in, kernels_in, mixing_in, bin_in, count_in, obs_in, isig_in,
            base, fields, stars, sums, mixing,
            turned, halves, coarse, kernels, star_bin, star_count, star_obs, star_isig, arrived):
    shard = lax.axis_index("rad")
    here = pl.ds(pl.multiple_of(shard * 128, 128), 128)
    moves = [(bin_in, star_bin), (count_in, star_count), (obs_in, star_obs), (isig_in, star_isig)]
    for i in range(2):
        for side in range(2):
            moves.append((excite_in.at[i, :, 128 * side : 128 * side + 128], halves.at[i, side]))
    moves += [(mixing_in.at[:, :, here], mixing), (coarse_in, coarse), (kernels_in.at[9:18, :, here], kernels)]
    moves = [pltpu.make_async_copy(a, b, arrived.at[n]) for n, (a, b) in enumerate(moves)]
    for move in moves:
        move.start()
    for move in moves[:4]:
        move.wait()

    def joined(x):
        return jnp.concatenate([x[0], x[1]], axis=1)

    count = jnp.concatenate([star_count[0:1, :], star_count[1:2, :]], axis=1)
    rel = joined(star_bin) - 256 * shard
    live = (rows((16, 128)) < count) & (rel >= 0) & (rel < 256)
    isig = joined(star_isig)
    w = jnp.where(live, isig * isig, 0.0)
    o = w * joined(star_obs)
    rel = jnp.where(live, rel, -1)
    hits = [[[], []], [[], []]]
    for tile in range(16):
        bin0 = 2 * (rows((8, 128)) + 8 * tile)
        bin1 = bin0 + 1
        total = [[jnp.zeros((8, 128), F32)] * 2 for _ in range(2)]
        for m in range(16):
            at = rel[m : m + 1, :]
            for k, bins in ((0, bin0), (1, bin1)):
                here_now = at == bins
                for f, value in ((0, w), (1, o)):
                    total[f][k] = total[f][k] + jnp.where(here_now, value[m : m + 1, :], 0.0)
        for f in range(2):
            for k in range(2):
                hits[f][k].append(total[f][k])
    hits = [[jnp.concatenate(hits[f][k], axis=0) for k in range(2)] for f in range(2)]
    pairs = jnp.concatenate([hits[f][0] + hits[f][1] for f in range(2)], axis=1)
    beyond = (lanes((128, 128)) > rows((128, 128))).astype(F32)
    after = jnp.dot(beyond, pairs, precision=HI, preferred_element_type=F32)
    ends = []
    for f in range(2):
        second = after[:, 128 * f : 128 * f + 128] + hits[f][1]
        first = second + hits[f][0]
        for k, value in ((0, first), (1, second)):
            stars[2 + 2 * f + k] = value.T
            ends.append((40 + 16 * f + k, value[0:1, :]))
            ends.append((48 + 16 * f + k, value[127:128, :]))
    for k in range(2):
        stars[k] = hits[0][k].T
    row = rows((8, 128))
    groups = [jnp.zeros((8, 128), F32)] * 16
    for at, value in ends:
        groups[at // 8] = jnp.where(row == at % 8, value, groups[at // 8])
    turned[...] = jnp.concatenate(groups, axis=0).T
    table = jnp.zeros((32, 128), F32)
    for p in range(4):
        table = table + pltpu.roll(turned[pixels(p), :], 2 * p, 1)
    sums[...] = table
    for move in moves[4:]:
        move.wait()
    parts = []
    for i in range(2):
        for j in range(2):
            parts += split_pixels(halves.at[i], j)
    for p in range(8):
        fields[p] = parts[p]
    acc = []
    for q in range(8):
        block = mixing[q]
        total = block[0:1, :] * parts[0]
        for p in range(1, 8):
            total = total + block[p : p + 1, :] * parts[p]
        acc.append(total)
    taps(acc, coarse[...], [kernels[t] for t in range(9)])
    for q in range(8):
        base[q] = acc[q]


def sides(odd, even):
    first = (lax.axis_index("ang") & 1) == 0
    return jnp.where(first, odd, even), jnp.where(first, even, odd)


def even_side():
    return 2 * (1 - (lax.axis_index("ang") & 1))


def even_row(coarse, first_hop, last_hop, base, kernels, sums, base_out, sums_out):
    u = even_side()
    here = pl.ds(pl.multiple_of(lax.axis_index("rad") * 128, 128), 128)
    even = jnp.where(lax.axis_index("ang") % 4 < 2, first_hop[...], last_hop[...])
    acc = [base[q] for q in range(8)]
    taps(acc, even, [kernels[9 * u + t, :, here] for t in range(9)])
    for q in range(8):
        base_out[q] = acc[q]
    lane = lanes((32, 128))
    out = sums[...]
    for at, value in ((1, coarse[...]), (u, even)):
        out = jnp.where(lane == 32 + at, value[:, 0:1], out)
        out = jnp.where(lane == 35 + at, value[:, 127:128], out)
    sums_out[...] = out


def forward(odd, base, kernels, stars, sums, dens, table):
    shard = lax.axis_index("rad")
    step = 1.0 / 1024
    acc = [base[q] for q in range(8)]
    place = lax.axis_index("ang")
    met = (place > 0) & (place < lax.axis_size("ang") - 1)
    row = jnp.where(met, odd[...], 0.0)
    u = 2 - even_side()
    here = pl.ds(pl.multiple_of(shard * 128, 128), 128)
    taps(acc, row, [kernels[9 * u + t, :, here] for t in range(9)])
    lane = lanes((32, 128))
    out = sums[...]
    for q in range(8):
        out = jnp.where(lane == q, acc[q][:, 0:1], out)
        out = jnp.where(lane == 8 + q, acc[q][:, 127:128], out)
    out = jnp.where(lane == 32 + u, row[:, 0:1], out)
    out = jnp.where(lane == 35 + u, row[:, 127:128], out)
    inner = (lane > 0) & (lane < 127)
    density = []
    for q in range(8):
        d = jnp.exp(acc[q])
        dens[q] = d
        density.append(jnp.where(inner, d, 0.0))
    for p in range(4):
        first, second = density[2 * p], density[2 * p + 1]
        share = weighed(first, stars[2, pixels(p), :]) + weighed(second, stars[3, pixels(p), :])
        total = jnp.sum(first + second, axis=1, keepdims=True)
        share = step * jnp.sum(share, axis=1, keepdims=True)
        for k in range(2):
            out = jnp.where(lane == 16 + 2 * p + k, total, out)
            out = jnp.where(lane == 24 + 2 * p + k, share, out)
    table[...] = out


def weighed(x, w):
    return jnp.where(w != 0.0, x * w, 0.0)


def swap(x):
    even = (rows(x.shape) & 1) == 0
    return jnp.where(even, pltpu.roll(x, x.shape[0] - 1, 0), pltpu.roll(x, 1, 0))


def spread(grad, columns):
    lane = lanes((32, 128))
    plus, minus = [], []
    for q in range(8):
        plus.append(jnp.where(lane == 127, columns[:, 32 + q : 33 + q], grad[q]))
        minus.append(jnp.where(lane == 0, columns[:, 40 + q : 41 + q], grad[q]))
    return minus, grad, plus


def to_row(u, fields, kernels, shard):
    at = pl.ds(pl.multiple_of(shard * 128, 128), 128)
    prev = pl.ds(pl.multiple_of(jnp.maximum(shard - 1, 0) * 128, 128), 128)
    after = pl.ds(pl.multiple_of(jnp.minimum(shard + 1, 3) * 128, 128), 128)
    lane = lanes((8, 128))
    total = None
    for w, field in enumerate(fields):
        part = None
        for v in range(3):
            t = 9 * u + 3 * v + w
            block = kernels[t, :, at]
            if w == 0:
                block = jnp.where(lane == 0, kernels[t, :, after], block)
            if w == 2:
                block = jnp.where(lane == 127, kernels[t, :, prev], block)
            piece = block[0:1, :] * field[0]
            for q in range(1, 8):
                piece = piece + block[q : q + 1, :] * field[q]
            piece = along(piece, 1 - v, 0)
            part = piece if part is None else part + piece
        if w != 1:
            part = pltpu.roll(part, (w - 1) % 128, 1)
        total = part if total is None else total + part
    return total


def middle(dens, stars, kernels, share, weights):
    step = 1.0 / 1024
    lane = lanes((32, 128))
    inner = (lane > 0) & (lane < 127)
    density = [jnp.where(inner, dens[q], 0.0) for q in range(8)]
    pairs = jnp.concatenate([density[2 * p] + density[2 * p + 1] for p in range(4)], axis=0)
    strict = (rows((128, 128)) < lanes((128, 128))).astype(F32)
    before = jnp.dot(pairs, strict, precision=HI, preferred_element_type=F32)
    prod = []
    for p in range(4):
        first = before[32 * p : 32 * p + 32] + density[2 * p]
        second = first + density[2 * p + 1]
        prod.append(weighed(step * first, stars[0, pixels(p), :]))
        prod.append(weighed(step * second, stars[1, pixels(p), :]))
    pairs = jnp.concatenate([prod[2 * p] + prod[2 * p + 1] for p in range(4)], axis=0)
    beyond = (rows((128, 128)) > lanes((128, 128))).astype(F32)
    after = jnp.dot(pairs, beyond, precision=HI, preferred_element_type=F32)
    for p in range(4):
        second = after[32 * p : 32 * p + 32] + prod[2 * p + 1]
        first = second + prod[2 * p]
        for k, value in ((0, first), (1, second)):
            share[2 * p + k] = value - stars[4 + k, pixels(p), :]
    for s in range(4):
        for n in range(9):
            for side in range(2):
                block = kernels[3 * n + 2 * side, :, 128 * s : 128 * s + 128]
                weights[s, side, n] = jnp.broadcast_to(block[:, 127 * side : 127 * side + 1], (8, 128))


def backward(own, by1, by2, by3, dens, share, weights, kernels, stars, grad, edges_out, odd_out, even_out):
    shard = lax.axis_index("rad")
    step = 1.0 / 1024
    even = (rows((8, 128)) & 1) == 0
    held = [own[...], by1[...], by2[...], by3[...]]
    groups = []
    for s in range(4):
        table = held[0]
        for k in range(1, 4):
            table = jnp.where(shard == (s ^ k), held[k], table)
        full = jnp.concatenate([table, jnp.zeros((96, 128), F32)], axis=0).T
        groups.append([full[8 * g : 8 * g + 8] for g in range(9)])
    edges = []
    for s in range(4):
        e = groups[s][4]
        edges.append([along(e, v - 1, 1) for v in range(3)])
    d_low, d_high, totals, shares, whole, tails = [], [], [], [], [], []
    for s in range(4):
        f_low, f_high, t, c, _, w_low, w_high, o_low, _ = groups[s]
        for u in range(3):
            for v in range(3):
                if s > 0:
                    f_low = f_low + weights[s, 0, 3 * u + v] * edges[s - 1][v][3 + u : 4 + u, :]
                if s < 3:
                    f_high = f_high + weights[s, 1, 3 * u + v] * edges[s + 1][v][u : u + 1, :]
        a, b = jnp.exp(f_low), jnp.exp(f_high)
        d_low.append(a)
        d_high.append(b)
        both = a + b
        totals.append(t + both + swap(both))
        tail = step * b * w_high
        tail = tail + swap(tail)
        tails.append(tail)
        head = step * a * w_low
        o_all = jnp.where(even, o_low, swap(o_low))
        shares.append(c - o_all + head + swap(head) + tail)
        whole.append(jnp.where(even, w_low, swap(w_low)))
    zero = jnp.zeros((8, 128), F32)
    nearer = [zero]
    for s in range(3):
        nearer.append(nearer[s] + totals[s])
    nearer = [step * x for x in nearer]
    sums = [shares[s] + weighed(nearer[s], whole[s]) for s in range(4)]
    farther = [zero]
    for s in (3, 2, 1):
        farther.insert(0, farther[0] + sums[s])

    def low_edge(s):
        w, o = groups[s][5], groups[s][7]
        first = weighed(nearer[s] + step * swap(d_low[s]), swap(w) - w) - (swap(o) - o)
        suffix = sums[s] - jnp.where(even, 0.0, first)
        return d_low[s] * step * (farther[s] + suffix)

    def high_edge(s):
        w, o = groups[s][6], groups[s][8]
        last = step * swap(d_high[s]) * (w - swap(w))
        suffix = weighed(nearer[s] + step * totals[s], w) - o - jnp.where(even, last, 0.0)
        return d_high[s] * step * (farther[s] + suffix)

    def mine(values):
        out = values[0]
        for s in range(1, 4):
            out = jnp.where(shard == s, values[s], out)
        return out

    lows = [low_edge(s) for s in range(4)]
    highs = [high_edge(s) for s in range(4)]
    columns = [mine(lows), mine(highs),
               mine([nearer[s] + step * (d_low[s] + swap(d_low[s])) for s in range(4)]),
               mine([farther[s] + tails[s] for s in range(4)]),
               mine([zero] + highs[:3]), mine(lows[1:] + [zero])]
    columns = jnp.concatenate(columns + [jnp.zeros((80, 128), F32)], axis=0).T[0:32]
    edges_out[...] = columns
    lane = lanes((32, 128))
    grads = []
    for p in range(4):
        near, far = columns[:, 16 + 2 * p : 17 + 2 * p], columns[:, 24 + 2 * p : 25 + 2 * p]
        for k in range(2):
            q = 2 * p + k
            suffix = far + weighed(near, stars[2 + k, pixels(p), :]) + share[q]
            g = step * dens[q] * suffix
            g = jnp.where(lane == 0, columns[:, q : q + 1], g)
            g = jnp.where(lane == 127, columns[:, 8 + q : 9 + q], g)
            grad[q] = g
            grads.append(g)
    fields = spread(grads, columns)
    odd, even_row = sides(to_row(0, fields, kernels, shard), to_row(2, fields, kernels, shard))
    odd_out[...] = odd
    even_out[...] = even_row


def finish(grad, columns, fields, kernels, mixing, out, own, halves):
    shard = lax.axis_index("rad")
    lane = lanes((32, 128))
    grads = [grad[q] for q in range(8)]
    acc = [fields[p] for p in range(8)]
    for q in range(8):
        block = mixing[q]
        for p in range(8):
            acc[p] = acc[p] + block[p : p + 1, :] * grads[q]
    for i in range(2):
        for j in range(2):
            pair = acc[4 * i + 2 * j : 4 * i + 2 * j + 2]
            half = pl.ds(j, 32, stride=2)
            for side in range(2):
                index = (lane >> 1) + 64 * side
                value = jnp.where((lane & 1) == 0, pick(pair[0], index), pick(pair[1], index))
                halves[side, half, :] = value
        for side in range(2):
            out[i, :, 128 * side : 128 * side + 128] = halves[side]
    own[...] = to_row(1, spread(grads, columns[...]), kernels, shard)


def total(own, even, odd, out):
    place = lax.axis_index("ang")
    met = (place > 0) & (place < lax.axis_size("ang") - 1)
    out[...] = own[...] + even[...] + jnp.where(met, odd[...], 0.0)


def call(body, ins, outs, flops, scratch=(), space=pltpu.VMEM):
    shapes = tuple(jax.ShapeDtypeStruct(s, d) for s, d in outs)
    size = sum(x.size * 4 for x in ins) + sum(x.size * 4 for x in shapes)
    return pl.pallas_call(
        body,
        out_shape=shapes,
        in_specs=[pl.BlockSpec(memory_space=space)] * len(ins),
        out_specs=tuple([VMEM] * len(shapes)),
        scratch_shapes=list(scratch),
        cost_estimate=pl.CostEstimate(flops=flops, bytes_accessed=size, transcendentals=0),
        compiler_params=pltpu.CompilerParams(vmem_limit_bytes=16 << 20),
    )(*ins)


def per_device(coarse, excite, kernels, mixing, star_bin, star_count, star_obs, star_isig):
    count = lax.axis_size("ang")
    pairs = [[], []]
    for i in range(count - 1):
        pairs[i % 2] += [(i, i + 1), (i + 1, i)]

    near = lax.axis_size("rad")
    hops = [(a * near + r, b * near + r) for a, b in pairs[1] for r in range(near)]
    hops += [(a * near + r, a * near + (r ^ 1)) for a in (0, count - 1) for r in range(near)]
    own = coarse[0, 0]

    def part(keep):
        hops = []
        for a in range(count):
            b = a ^ 1
            hops += [(a * near + r, b * near + r if keep(a % 4) else a * near + (r ^ 1)) for r in range(near)]
        return hops

    first = lax.ppermute(own, ("ang", "rad"), part(lambda z: z < 2))
    odd = lax.ppermute(own, ("ang", "rad"), hops)
    last = lax.ppermute(own, ("ang", "rad"), part(lambda z: z >= 2))
    block = ((8, 32, 128), F32)
    row = ((32, 128), F32)
    stars = [x.transpose(0, 2, 1) for x in (star_bin, star_obs, star_isig)]
    base, fields, stars, sums, mixing_here = call(
        prepare,
        [pltpu.with_memory_space_constraint(x, pltpu.HBM) for x in
         (own, excite[0], kernels, mixing, stars[0], star_count, stars[1], stars[2])],
        (block, block, ((6, 128, 128), F32), row, ((8, 8, 128), F32)), 4_000_000,
        [pltpu.VMEM((128, 128), F32), pltpu.VMEM((2, 2, 64, 128), F32), pltpu.VMEM((32, 128), F32),
         pltpu.VMEM((9, 8, 128), F32), pltpu.VMEM((2, 16, 64), jnp.int32), pltpu.VMEM((2, 64), jnp.int32),
         pltpu.VMEM((2, 16, 64), F32), pltpu.VMEM((2, 16, 64), F32), pltpu.SemaphoreType.DMA((11,))],
        pltpu.HBM,
    )
    base, sums = call(even_row, (own, first, last, base, kernels, sums), (block, row), 3_000_000)
    dens, table = call(
        forward, (odd, base, kernels, stars, sums),
        (block, row), 6_000_000,
    )
    others = [lax.ppermute(table, "rad", [(i, i ^ k) for i in range(4)]) for k in (1, 2, 3)]
    share, weights = call(
        middle, (dens, stars, kernels), (block, ((4, 2, 9, 8, 128), F32)), 1_000_000,
    )
    grad, columns, odd, even = call(
        backward, (table, *others, dens, share, weights, kernels, stars),
        (block, row, row, row), 8_000_000,
    )
    even = lax.ppermute(even, "ang", pairs[0])
    odd = lax.ppermute(odd, ("ang", "rad"), hops)
    grad_excite, here = call(
        finish, (grad, columns, fields, kernels, mixing_here),
        (((2, 64, 256), F32), row), 4_000_000,
        [pltpu.VMEM((2, 64, 128), F32)],
    )
    (grad_coarse,) = call(total, (here, even, odd), (row,), 10_000)
    return grad_excite[None], grad_coarse[None, None]


def solution(mesh):
    in_specs = (
        P(None, "ang", None, "rad"),
        P(None, "ang", None, "rad"),
        P(),
        P(),
        P("ang", None, None),
        P("ang", None),
        P("ang", None, None),
        P("ang", None, None),
    )
    out_specs = (P(None, "ang", None, "rad"), P(None, "ang", None, "rad"))
    return jax.shard_map(
        per_device, mesh=mesh, in_specs=in_specs, out_specs=out_specs, check_vma=False
    )
```
